256 devices in a mesh: wall: 16 (over y, x_lo, core), span: 16 (over x_hi, z).
Axes of the slice: x: 4 (x_hi: 2, x_lo: 2; x = x_hi * 2 + x_lo), y: 4, z: 8, core: 2. Of those that a mesh axis runs over, the one named last changes fastest.
Arguments:
- field: float32 [4, 3, 2, 512, 6144], P(None, None, None, 'wall', 'span'), may hold values from -6 to 6
- mean_flow: float32 [2, 512], P(None, 'wall'), may hold values from 0.2 to 1.5
- d2_coef: float32 [15, 512], P(None, 'wall'), may hold values from -2 to 2
- wall_coef: float32 [2, 8], replicated, may hold values from -0.4375 to 0.4375
- kx_index: int32 [4], replicated, may hold values from 1 to 7
- patch_of: int32 [6144], P('span'), may hold values from 0 to 63
Outputs:
- new_field: float32 [4, 3, 2, 512, 6144], P(None, None, None, 'wall', 'span')
- wall_grad: float32 [2, 4, 2, 64], replicated
The draws below stay inside these ranges and needn't reach their ends.
All inputs are finite; a program needn't handle non-finite values.
Results may differ from the reference program's by a relative error of at most 0.000073.
Values sent between devices are 32-bit elements; how exact they have to be, the bound alone decides.
A program may use at most 128 MiB of HBM per device.

```python
import jax
import jax.numpy as jnp
from jax import lax

KX = 4
NZ = 6144
NY = 512
HALO = 7
STEN = 15
PATCH = 64


def set_ends(values, own_key, low, largest):
    longest = values.shape.index(max(values.shape))
    spots = []
    for shift in (0, 1):
        where = [jax.random.randint(jax.random.fold_in(own_key, axis), (), 0, length) for axis, length in enumerate(values.shape)]
        where[longest] = (where[longest] + shift) % values.shape[longest]
        spots.append(tuple(where))
    return values.at[spots[0]].set(low).at[spots[1]].set(largest)


def level_of(own_key, dims, cuts, least, largest):
    factor_of, own = 1.0, jax.random.fold_in(own_key, 6)
    for position, shards_of in cuts:
        draws = jnp.exp(jax.random.uniform(jax.random.fold_in(own, position), (shards_of,), jnp.float32, least / len(cuts), largest / len(cuts)))
        factor_of = factor_of * jnp.repeat(draws, dims[position] // shards_of).reshape([-1 if axis == position else 1 for axis in range(len(dims))])
    return factor_of


def noise(key, shape, spread, most, shards=(), kind=jnp.bfloat16):
    level = level_of(key, shape, shards, -0.22, 0.18) if shards else 1.0
    array = jax.random.normal(key, shape, jnp.float32) * spread * level
    return jnp.minimum(jnp.maximum(array, -most), most).astype(kind)


def setup_inputs(seed: int = 0) -> dict:
    arg_keys = jax.random.split(jax.random.key(seed), 7)
    return {
        "field": noise(arg_keys[0], (KX, 3, 2, NY, NZ), 1.0, 6.0, ((3, 16), (4, 16)), jnp.float32),
        "mean_flow": jnp.clip(0.2 + 1.3 * jax.random.uniform(arg_keys[1], (2, NY), jnp.float32) ** level_of(arg_keys[1], (2, NY), ((1, 16),), -0.2, 0.2), 0.2, 1.5),
        "d2_coef": noise(arg_keys[2], (STEN, NY), 0.15, 2.0, ((1, 16),), jnp.float32),
        "wall_coef": noise(arg_keys[3], (2, HALO + 1), 0.03, 0.4375, (), jnp.float32),
        "kx_index": set_ends(jax.random.randint(arg_keys[4], (KX,), 1, 8), jax.random.fold_in(arg_keys[4], 1), 1, 7).astype(jnp.int32),
        "patch_of": set_ends(jax.random.randint(arg_keys[5], (NZ,), 0, PATCH), jax.random.fold_in(arg_keys[5], 1), 0, PATCH - 1).astype(jnp.int32),
    }


TAU = 0.25
VIS = 0.5


def reference(field, mean_flow, d2_coef, wall_coef, kx_index, patch_of):
    wave_number = kx_index.astype(jnp.float32) * 0.25
    padded = jnp.pad(field, ((0, 0), (0, 0), (0, 0), (HALO, HALO), (0, 0)))
    diffusion = jnp.zeros_like(field)
    for offset in range(STEN):
        diffusion = diffusion + d2_coef[offset][:, None] * padded[:, :, :, offset:offset + NY, :]
    complex_field = field[:, :, 0] + 1j * field[:, :, 1]
    spectrum = jnp.fft.fft(complex_field, axis=-1)
    frequency = jnp.arange(NZ, dtype=jnp.int32)
    signed = jnp.where(frequency > NZ // 2, frequency - NZ, frequency)
    cutoff = NZ // 3
    wave_ratio = signed.astype(jnp.float32) / cutoff
    multiplier = jnp.where(jnp.abs(signed) < cutoff, -VIS * wave_ratio * wave_ratio, 0.0 * wave_ratio)
    returned = jnp.fft.ifft(spectrum * multiplier, axis=-1)
    spanwise = jnp.stack([jnp.real(returned), jnp.imag(returned)], axis=2).astype(field.dtype)
    velocity = mean_flow[0]
    shear_rate = mean_flow[1]
    advect_rate = wave_number[:, None, None, None] * velocity[None, None, :, None]
    advect_real = -advect_rate * field[:, :, 1]
    advect_imag = advect_rate * field[:, :, 0]
    advection = jnp.stack([advect_real, advect_imag], axis=2)
    coupling = shear_rate[None, None, :, None] * field[:, 0]
    advection = advection.at[:, 1].add(-coupling)
    new_field = field + TAU * advection + diffusion + spanwise
    lower_wall = jnp.zeros_like(new_field[:, 0, :, 0, :])
    upper_wall = jnp.zeros_like(new_field[:, 0, :, 0, :])
    for offset in range(HALO + 1):
        lower_wall = lower_wall + wall_coef[0, offset] * new_field[:, 0, :, offset, :]
        upper_wall = upper_wall + wall_coef[1, offset] * new_field[:, 0, :, NY - 1 - offset, :]
    shear_rows = jnp.stack([lower_wall, upper_wall])
    onehot = (patch_of[:, None] == jnp.arange(PATCH, dtype=jnp.int32)[None, :]).astype(field.dtype)
    wall_grad = jnp.einsum("wmcz,zp->wmcp", shear_rows, onehot, precision=lax.Precision.HIGHEST)
    return new_field, wall_grad
```

```python
import math

import jax
import jax.numpy as jnp
import numpy as np
from jax import lax
from jax.experimental import pallas as pl
from jax.experimental.pallas import tpu as pltpu
from jax.sharding import PartitionSpec as P

MESH = pl.DeviceIdType.MESH
MODES, COMPS, ROWS, COLS = 4, 3, 32, 384
WALLS, SPANS = 16, 16
STEN = 15
PATCH = 64
NZ = SPANS * COLS
INNER = 128
OUTER = NZ // INNER
CUTOFF = NZ // 3
VIS = 0.5
TAU = 0.25

OFFSETS = sorted(
    [(hi, z) for hi in range(2) for z in range(8) if hi or z],
    key=lambda o: (2 * o[0] + min(o[1], 8 - o[1]), o),
)


def tables():
    outer = np.array([next(k for k in range(OUTER) if k % 16 == i // 3 and k % 3 == i % 3) for i in range(OUTER)])
    inner = np.arange(INNER)
    angle = 2.0 * np.pi * (outer[:, None] * inner[None, :] % NZ) / NZ
    twist = np.stack([np.cos(angle), np.sin(angle)], axis=1)
    wave = outer[:, None] + OUTER * inner[None, :]
    signed = np.where(wave > NZ // 2, wave - NZ, wave)
    factor = np.where(np.abs(signed) < CUTOFF, -VIS * (signed / CUTOFF) ** 2, 0.0) / NZ
    angle = 2.0 * np.pi * (inner[:, None] * inner[None, :] % INNER) / INNER
    c, s = np.cos(angle), np.sin(angle)
    pair = []
    for table in (np.block([[c, -s], [s, c]]), np.block([[c, s], [-s, c]])):
        high = table.astype(np.float32).astype(jnp.bfloat16)
        low = (table - high.astype(np.float64)).astype(np.float32).astype(jnp.bfloat16)
        pair.append(np.stack([high, low]))
    rows = np.concatenate([twist, factor[:, None]], axis=1).astype(np.float32)
    return np.stack(pair), rows


def times(value, cos, sin):
    re, im = value
    half = math.sqrt(0.5)
    if abs(sin) < 1e-12:
        return (re, im) if cos > 0 else (-re, -im)
    if abs(cos) < 1e-12:
        return (im, -re) if sin > 0 else (-im, re)
    if abs(abs(cos) - half) < 1e-12 and abs(abs(sin) - half) < 1e-12:
        a, b = math.copysign(half, cos), math.copysign(half, sin)
        if a == b:
            return ((re + im) * a, (im - re) * a)
        return ((re - im) * a, (im + re) * a)
    return (re * cos + im * sin, im * cos - re * sin)


def transform(values):
    n = len(values)
    if n == 1:
        return values
    even, odd = transform(values[0::2]), transform(values[1::2])
    first, second = [], []
    for k in range(n // 2):
        a = 2.0 * math.pi * k / n
        t = times(odd[k], math.cos(a), math.sin(a))
        first.append((even[k][0] + t[0], even[k][1] + t[1]))
        second.append((even[k][0] - t[0], even[k][1] - t[1]))
    return first + second


def transform_three(x):
    (ar, ai), (br, bi), (cr, ci) = x
    sr, si, dr, di = br + cr, bi + ci, br - cr, bi - ci
    mr, mi = ar - 0.5 * sr, ai - 0.5 * si
    h = math.sqrt(0.75)
    return [(ar + sr, ai + si), (mr + h * di, mi - h * dr), (mr - h * di, mi + h * dr)]


def swap(values):
    return [(im, re) for re, im in values]


def multiply(values, pair_ref, which):
    high = values.astype(jnp.bfloat16)
    low = (values - high.astype(jnp.float32)).astype(jnp.bfloat16)
    out = jnp.dot(high, pair_ref[which, 0], preferred_element_type=jnp.float32)
    out += jnp.dot(low, pair_ref[which, 0], preferred_element_type=jnp.float32)
    out += jnp.dot(high, pair_ref[which, 1], preferred_element_type=jnp.float32)
    return out


def filter_lines(c, recv, ret, work, mid, pair, trig):
    def lanes(j):
        return slice(INNER * j, INNER * (j + 1))

    for j in range(3):
        order = [(i + 5 * j) % 16 for i in range(16)]
        out = transform([(recv[c, s, 0, :, lanes(j)], recv[c, s, 1, :, lanes(j)]) for s in order])
        for k in range(16):
            work[3 * k + j, :, :INNER], work[3 * k + j, :, INNER:] = out[k]
    for k in range(16):
        out = transform_three([(work[3 * k + j, :, :INNER], work[3 * k + j, :, INNER:]) for j in range(3)])
        for i, (re, im) in enumerate(out):
            cos, sin = trig[3 * k + i, 0:1, :], trig[3 * k + i, 1:2, :]
            mid[3 * k + i, :, :INNER] = re * cos + im * sin
            mid[3 * k + i, :, INNER:] = im * cos - re * sin
    modes = multiply(mid[...].reshape(OUTER * 8, 2 * INNER), pair, 0).reshape(OUTER, 8, 2 * INNER)
    work[...] = modes
    for k in range(OUTER):
        factor = trig[k, 2:3, :]
        mid[k, :, :INNER] = work[k, :, :INNER] * factor
        mid[k, :, INNER:] = work[k, :, INNER:] * factor
    work[...] = multiply(mid[...].reshape(OUTER * 8, 2 * INNER), pair, 1).reshape(OUTER, 8, 2 * INNER)
    for k in range(16):
        values = []
        for i in range(3):
            re, im = work[3 * k + i, :, :INNER], work[3 * k + i, :, INNER:]
            cos, sin = trig[3 * k + i, 0:1, :], trig[3 * k + i, 1:2, :]
            values.append((re * cos - im * sin, im * cos + re * sin))
        out = swap(transform_three(swap(values)))
        for j in range(3):
            mid[3 * k + j, :, :INNER], mid[3 * k + j, :, INNER:] = out[j]
    for j in range(3):
        order = [(i + 5 * j) % 16 for i in range(16)]
        out = swap(transform(swap([(mid[3 * k + j, :, :INNER], mid[3 * k + j, :, INNER:]) for k in range(16)])))
        for i, s in enumerate(order):
            ret[c, s, 0, :, lanes(j)], ret[c, s, 1, :, lanes(j)] = out[i]


def local_terms(c, padded, base, coef, wave_ref):
    def body(i, carry):
        m, j = i // 3, i % 3
        lanes = pl.ds(pl.multiple_of(j * INNER, INNER), INNER)
        rate = TAU * 0.25 * wave_ref[m].astype(jnp.float32)
        for octet in range(ROWS // 8):
            rows = slice(8 * octet, 8 * octet + 8)
            sums = []
            for p in range(2):
                total = jnp.zeros((8, INNER), jnp.float32)
                for s in range(STEN):
                    total += coef[s, rows, :] * padded[m, c, p, 8 * octet + 1 + s : 8 * octet + 9 + s, lanes]
                sums.append(total)
            here = slice(8 * octet + 8, 8 * octet + 16)
            re, im = padded[m, c, 0, here, lanes], padded[m, c, 1, here, lanes]
            turn = rate * coef[STEN, rows, :]
            sums[0] += re - turn * im
            sums[1] += im + turn * re
            if c == 1:
                couple = TAU * coef[STEN + 1, rows, :]
                for p in range(2):
                    sums[p] -= couple * padded[m, 0, p, here, lanes]
            for p in range(2):
                base[m, c, p, rows, lanes] = sums[p]
        return carry

    lax.fori_loop(0, MODES * 3, body, 0)


def kernel(
    field, mean_flow, d2_coef, wall_coef, kx_index, patch_of, pair_hbm, trig_hbm,
    base_out, spw, grad_out,
    padded, base, recv, ret, work, mid, pair, trig, coef, turned, flow, sten, wc, kx, patch, edge, grads, shares,
    load_sem, own_sem, back_sem, f_send, f_recv, r_send, r_recv, h_send, h_recv, s_send, s_recv, g_send, g_recv,
    out_sem, edge_sem,
):
    w, me = lax.axis_index("wall"), lax.axis_index("span")
    at_low, at_high = w == 0, w == WALLS - 1
    at_edge = jnp.logical_or(at_low, at_high)

    def span_of(offset, sign=1):
        hi = lax.rem(me // 8 + offset[0], 2)
        return hi * 8 + lax.rem(lax.rem(me, 8) + 8 + sign * offset[1], 8)

    loads = [
        pltpu.make_async_copy(field, padded.at[:, :, :, pl.ds(8, ROWS), :], load_sem.at[0]),
        pltpu.make_async_copy(mean_flow, flow, load_sem.at[1]),
        pltpu.make_async_copy(d2_coef, sten, load_sem.at[2]),
        pltpu.make_async_copy(wall_coef, wc, load_sem.at[3]),
        pltpu.make_async_copy(kx_index, kx, load_sem.at[4]),
        pltpu.make_async_copy(patch_of, patch, load_sem.at[5]),
        pltpu.make_async_copy(pair_hbm, pair, load_sem.at[6]),
        pltpu.make_async_copy(trig_hbm, trig, load_sem.at[7]),
    ]

    barrier = pltpu.get_barrier_semaphore()
    for offset in OFFSETS:
        pl.semaphore_signal(barrier, inc=1, device_id=(w, span_of(offset)), device_id_type=MESH)

    def greet(wall):
        pl.semaphore_signal(barrier, inc=1, device_id=(wall, me), device_id_type=MESH)

    pl.when(w > 0)(lambda: greet(w - 1))
    pl.when(w < WALLS - 1)(lambda: greet(w + 1))
    pl.when(w > 1)(lambda: greet(0))
    pl.when(w < WALLS - 2)(lambda: greet(WALLS - 1))
    for load in loads:
        load.start()
    pl.when(at_edge)(lambda: pl.semaphore_wait(barrier, SPANS - 1 + WALLS - 1))
    pl.when(jnp.logical_not(at_edge))(lambda: pl.semaphore_wait(barrier, SPANS - 1 + 2))

    def block(t, c):
        return (t // 4, c, slice(None), pl.ds(pl.multiple_of(8 * lax.rem(t, 4), 8), 8), slice(None))

    def forward(c, t, slot):
        return pltpu.make_async_remote_copy(
            src_ref=field.at[block(t, c)], dst_ref=recv.at[c, slot], send_sem=f_send.at[c, t],
            recv_sem=f_recv.at[c, slot], device_id=(w, t), device_id_type=MESH)

    def backward(c, t, slot):
        return pltpu.make_async_remote_copy(
            src_ref=ret.at[c, t], dst_ref=spw.at[block(slot, c)], send_sem=r_send.at[c, t],
            recv_sem=r_recv.at[c, slot], device_id=(w, t), device_id_type=MESH)

    def own(c):
        return pltpu.make_async_copy(field.at[block(me, c)], recv.at[c, me], own_sem.at[c])

    def own_back(c):
        return pltpu.make_async_copy(ret.at[c, me], spw.at[block(me, c)], back_sem.at[c])

    def send_lines(c):
        for offset in OFFSETS:
            forward(c, span_of(offset), me).start()
        own(c).start()

    def take_lines(c):
        for offset in OFFSETS:
            forward(c, me, span_of(offset, -1)).wait_recv()
        own(c).wait()

    def send_back(c):
        for offset in OFFSETS:
            backward(c, span_of(offset), me).start()
        own_back(c).start()

    def take_back(c):
        for offset in OFFSETS:
            backward(c, me, span_of(offset, -1)).wait_recv()
        own_back(c).wait()

    def halo(up):
        src = pl.ds(ROWS - 8 if up else 0, 8)
        dst = pl.ds(0 if up else ROWS + 8, 8)
        return pltpu.make_async_remote_copy(
            src_ref=field.at[:, :, :, src, :], dst_ref=padded.at[:, :, :, dst, :], send_sem=h_send.at[int(up)],
            recv_sem=h_recv.at[int(up)], device_id=(w + 1 if up else w - 1, me), device_id_type=MESH)

    send_lines(0)
    pl.when(w < WALLS - 1)(lambda: halo(True).start())
    pl.when(w > 0)(lambda: halo(False).start())
    send_lines(1)

    @pl.when(at_low)
    def _():
        padded[:, :, :, 0:8, :] = jnp.zeros((MODES, COMPS, 2, 8, COLS), jnp.float32)

    @pl.when(at_high)
    def _():
        padded[:, :, :, ROWS + 8 :, :] = jnp.zeros((MODES, COMPS, 2, 8, COLS), jnp.float32)

    for load in loads:
        load.wait()
    turned[...] = jnp.zeros((INNER, INNER), jnp.float32)
    turned[0:STEN, 0:ROWS] = sten[...]
    turned[STEN : STEN + 2, 0:ROWS] = flow[...]
    columns = turned[...].T
    for k in range(STEN + 2):
        coef[k] = jnp.broadcast_to(columns[0:ROWS, k : k + 1], (ROWS, INNER))

    pl.when(w > 0)(lambda: halo(True).wait_recv())
    pl.when(w < WALLS - 1)(lambda: halo(False).wait_recv())
    local_terms(0, padded, base, coef, kx)

    take_lines(0)
    filter_lines(0, recv, ret, work, mid, pair, trig)
    send_back(0)
    send_lines(2)

    local_terms(1, padded, base, coef, kx)
    take_lines(1)
    filter_lines(1, recv, ret, work, mid, pair, trig)

    def share(t, slot):
        return pltpu.make_async_remote_copy(
            src_ref=grads.at[2], dst_ref=shares.at[slot], send_sem=s_send.at[t], recv_sem=s_recv.at[slot],
            device_id=(w, t), device_id_type=MESH)

    take_back(0)

    @pl.when(at_edge)
    def _():
        rows = pl.ds(pl.multiple_of(jnp.where(at_low, 0, ROWS - 8), 8), 8)
        copy = pltpu.make_async_copy(spw.at[:, 0, :, rows, :], edge, edge_sem)
        copy.start()
        copy.wait()
        line = lax.broadcasted_iota(jnp.int32, (8, COLS), 0)
        weight = jnp.zeros((8, COLS), jnp.float32)
        for j in range(8):
            weight = jnp.where(line == j, jnp.where(at_low, wc[0, j], wc[1, 7 - j]), weight)
        patches = (lax.broadcasted_iota(jnp.int32, (INNER, COLS), 0) == patch[...]).astype(jnp.bfloat16)
        sums = []
        for m in range(MODES):
            for p in range(2):
                values = weight * (base[m, 0, p, rows, :] + edge[m, p])
                sums.append(jnp.sum(values, axis=0, keepdims=True))
        rest = jnp.concatenate(sums, axis=0)
        total = jnp.zeros((8, INNER), jnp.float32)
        for _ in range(3):
            part = rest.astype(jnp.bfloat16)
            rest = rest - part.astype(jnp.float32)
            total += lax.dot_general(part, patches, (((1,), (1,)), ((), ())), preferred_element_type=jnp.float32)
        grads[2] = total
        for offset in OFFSETS:
            share(span_of(offset), me).start()

    send_back(1)
    local_terms(2, padded, base, coef, kx)
    base_copy = pltpu.make_async_copy(base, base_out, out_sem.at[0])
    base_copy.start()
    take_lines(2)
    filter_lines(2, recv, ret, work, mid, pair, trig)

    def spread(side, t):
        return pltpu.make_async_remote_copy(
            src_ref=grads.at[side], dst_ref=grads.at[side], send_sem=g_send.at[t], recv_sem=g_recv.at[side],
            device_id=(t, me), device_id_type=MESH)

    @pl.when(at_edge)
    def _():
        for offset in OFFSETS:
            share(me, span_of(offset, -1)).wait_recv()
        shares[me] = grads[2]
        total = shares[0]
        for s in range(1, SPANS):
            total += shares[s]
        grads[jnp.where(at_low, 0, 1)] = total

    @pl.when(at_low)
    def _():
        for t in range(1, WALLS):
            spread(0, t).start()

    @pl.when(at_high)
    def _():
        for t in range(WALLS - 1):
            spread(1, t).start()

    send_back(2)
    take_back(1)
    pl.when(jnp.logical_not(at_low))(lambda: spread(0, w).wait_recv())
    pl.when(jnp.logical_not(at_high))(lambda: spread(1, w).wait_recv())
    grad_copy = pltpu.make_async_copy(grads.at[pl.ds(0, 2)], grad_out, out_sem.at[1])
    grad_copy.start()
    take_back(2)
    for c in range(COMPS):
        for offset in OFFSETS:
            forward(c, span_of(offset), me).wait_send()
            backward(c, span_of(offset), me).wait_send()
    pl.when(w < WALLS - 1)(lambda: halo(True).wait_send())
    pl.when(w > 0)(lambda: halo(False).wait_send())

    @pl.when(at_edge)
    def _():
        for offset in OFFSETS:
            share(span_of(offset), me).wait_send()

    @pl.when(at_low)
    def _():
        for t in range(1, WALLS):
            spread(0, t).wait_send()

    @pl.when(at_high)
    def _():
        for t in range(WALLS - 1):
            spread(1, t).wait_send()

    base_copy.wait()
    grad_copy.wait()


def on_device(field, mean_flow, d2_coef, wall_coef, kx_index, patch_of):
    pair, trig = tables()
    whole = (MODES, COMPS, 2, ROWS, COLS)
    dma = pltpu.SemaphoreType.DMA
    hbm = pl.BlockSpec(memory_space=pl.ANY)
    base, spanwise, grads = pl.pallas_call(
        kernel,
        out_shape=[
            jax.ShapeDtypeStruct(whole, jnp.float32),
            jax.ShapeDtypeStruct(whole, jnp.float32),
            jax.ShapeDtypeStruct((2, 8, INNER), jnp.float32),
        ],
        in_specs=[hbm] * 8,
        out_specs=[hbm] * 3,
        scratch_shapes=[
            pltpu.VMEM((MODES, COMPS, 2, ROWS + 16, COLS), jnp.float32),
            pltpu.VMEM(whole, jnp.float32),
            pltpu.VMEM((COMPS, SPANS, 2, 8, COLS), jnp.float32),
            pltpu.VMEM((COMPS, SPANS, 2, 8, COLS), jnp.float32),
            pltpu.VMEM((OUTER, 8, 2 * INNER), jnp.float32),
            pltpu.VMEM((OUTER, 8, 2 * INNER), jnp.float32),
            pltpu.VMEM((2, 2, 2 * INNER, 2 * INNER), jnp.bfloat16),
            pltpu.VMEM((OUTER, 3, INNER), jnp.float32),
            pltpu.VMEM((STEN + 2, ROWS, INNER), jnp.float32),
            pltpu.VMEM((INNER, INNER), jnp.float32),
            pltpu.VMEM((2, ROWS), jnp.float32),
            pltpu.VMEM((STEN, ROWS), jnp.float32),
            pltpu.SMEM((2, 8), jnp.float32),
            pltpu.SMEM((MODES,), jnp.int32),
            pltpu.VMEM((1, COLS), jnp.int32),
            pltpu.VMEM((MODES, 2, 8, COLS), jnp.float32),
            pltpu.VMEM((3, 8, INNER), jnp.float32),
            pltpu.VMEM((SPANS, 8, INNER), jnp.float32),
            dma((8,)),
            dma((COMPS,)),
            dma((COMPS,)),
            dma((COMPS, SPANS)),
            dma((COMPS, SPANS)),
            dma((COMPS, SPANS)),
            dma((COMPS, SPANS)),
            dma((2,)),
            dma((2,)),
            dma((SPANS,)),
            dma((SPANS,)),
            dma((WALLS,)),
            dma((2,)),
            dma((2,)),
            dma,
        ],
        compiler_params=pltpu.CompilerParams(collective_id=0, has_side_effects=True),
    )(field, mean_flow, d2_coef, wall_coef, kx_index, patch_of.reshape(1, COLS), pair, trig)
    new_field = base + spanwise
    wall_grad = grads[:, :, :PATCH].reshape(2, MODES, 2, PATCH)
    return new_field, wall_grad


def solution(mesh):
    return jax.shard_map(
        on_device,
        mesh=mesh,
        in_specs=(
            P(None, None, None, "wall", "span"),
            P(None, "wall"),
            P(None, "wall"),
            P(),
            P(),
            P("span"),
        ),
        out_specs=(P(None, None, None, "wall", "span"), P()),
        check_vma=False,
    )
```

```python
import math

import jax
import jax.numpy as jnp
import numpy as np
from jax import lax
from jax.experimental import pallas as pl
from jax.experimental.pallas import tpu as pltpu
from jax.sharding import PartitionSpec as P

MESH = pl.DeviceIdType.MESH
MODES, COMPS, ROWS, COLS = 4, 3, 32, 384
WALLS, SPANS = 16, 16
STEN = 15
PATCH = 64
NZ = SPANS * COLS
INNER = 128
OUTER = NZ // INNER
CUTOFF = NZ // 3
VIS = 0.5
TAU = 0.25

OFFSETS = sorted(
    [(hi, z) for hi in range(2) for z in range(8) if hi or z],
    key=lambda o: (2 * o[0] + min(o[1], 8 - o[1]), o),
)


def tables():
    outer = np.array([next(k for k in range(OUTER) if k % 16 == i // 3 and k % 3 == i % 3) for i in range(OUTER)])
    inner = np.arange(INNER)
    angle = 2.0 * np.pi * (outer[:, None] * inner[None, :] % NZ) / NZ
    twist = np.stack([np.cos(angle), np.sin(angle)], axis=1)
    wave = outer[:, None] + OUTER * inner[None, :]
    signed = np.where(wave > NZ // 2, wave - NZ, wave)
    factor = np.where(np.abs(signed) < CUTOFF, -VIS * (signed / CUTOFF) ** 2, 0.0) / NZ
    angle = 2.0 * np.pi * (inner[:, None] * inner[None, :] % INNER) / INNER
    c, s = np.cos(angle), np.sin(angle)
    pair = []
    for table in (np.block([[c, -s], [s, c]]), np.block([[c, s], [-s, c]])):
        high = table.astype(np.float32).astype(jnp.bfloat16)
        low = (table - high.astype(np.float64)).astype(np.float32).astype(jnp.bfloat16)
        pair.append(np.stack([high, low]))
    rows = np.concatenate([twist, factor[:, None]], axis=1).astype(np.float32)
    return np.stack(pair), rows


def times(value, cos, sin):
    re, im = value
    half = math.sqrt(0.5)
    if abs(sin) < 1e-12:
        return (re, im) if cos > 0 else (-re, -im)
    if abs(cos) < 1e-12:
        return (im, -re) if sin > 0 else (-im, re)
    if abs(abs(cos) - half) < 1e-12 and abs(abs(sin) - half) < 1e-12:
        a, b = math.copysign(half, cos), math.copysign(half, sin)
        if a == b:
            return ((re + im) * a, (im - re) * a)
        return ((re - im) * a, (im + re) * a)
    return (re * cos + im * sin, im * cos - re * sin)


def transform(values):
    n = len(values)
    if n == 1:
        return values
    even, odd = transform(values[0::2]), transform(values[1::2])
    first, second = [], []
    for k in range(n // 2):
        a = 2.0 * math.pi * k / n
        t = times(odd[k], math.cos(a), math.sin(a))
        first.append((even[k][0] + t[0], even[k][1] + t[1]))
        second.append((even[k][0] - t[0], even[k][1] - t[1]))
    return first + second


def transform_three(x):
    (ar, ai), (br, bi), (cr, ci) = x
    sr, si, dr, di = br + cr, bi + ci, br - cr, bi - ci
    mr, mi = ar - 0.5 * sr, ai - 0.5 * si
    h = math.sqrt(0.75)
    return [(ar + sr, ai + si), (mr + h * di, mi - h * dr), (mr - h * di, mi + h * dr)]


def swap(values):
    return [(im, re) for re, im in values]


def multiply(values, pair_ref, which):
    high = values.astype(jnp.bfloat16)
    low = (values - high.astype(jnp.float32)).astype(jnp.bfloat16)
    out = jnp.dot(high, pair_ref[which, 0], preferred_element_type=jnp.float32)
    out += jnp.dot(low, pair_ref[which, 0], preferred_element_type=jnp.float32)
    out += jnp.dot(high, pair_ref[which, 1], preferred_element_type=jnp.float32)
    return out


def filter_lines(c, recv, ret, work, mid, pair, trig):
    def lanes(j):
        return slice(INNER * j, INNER * (j + 1))

    for j in range(3):
        order = [(i + 5 * j) % 16 for i in range(16)]
        out = transform([(recv[c, s, 0, :, lanes(j)], recv[c, s, 1, :, lanes(j)]) for s in order])
        for k in range(16):
            work[3 * k + j, :, :INNER], work[3 * k + j, :, INNER:] = out[k]
    for k in range(16):
        out = transform_three([(work[3 * k + j, :, :INNER], work[3 * k + j, :, INNER:]) for j in range(3)])
        for i, (re, im) in enumerate(out):
            cos, sin = trig[3 * k + i, 0:1, :], trig[3 * k + i, 1:2, :]
            mid[3 * k + i, :, :INNER] = re * cos + im * sin
            mid[3 * k + i, :, INNER:] = im * cos - re * sin
    modes = multiply(mid[...].reshape(OUTER * 8, 2 * INNER), pair, 0).reshape(OUTER, 8, 2 * INNER)
    work[...] = modes
    for k in range(OUTER):
        factor = trig[k, 2:3, :]
        mid[k, :, :INNER] = work[k, :, :INNER] * factor
        mid[k, :, INNER:] = work[k, :, INNER:] * factor
    work[...] = multiply(mid[...].reshape(OUTER * 8, 2 * INNER), pair, 1).reshape(OUTER, 8, 2 * INNER)
    for k in range(16):
        values = []
        for i in range(3):
            re, im = work[3 * k + i, :, :INNER], work[3 * k + i, :, INNER:]
            cos, sin = trig[3 * k + i, 0:1, :], trig[3 * k + i, 1:2, :]
            values.append((re * cos - im * sin, im * cos + re * sin))
        out = swap(transform_three(swap(values)))
        for j in range(3):
            mid[3 * k + j, :, :INNER], mid[3 * k + j, :, INNER:] = out[j]
    for j in range(3):
        order = [(i + 5 * j) % 16 for i in range(16)]
        out = swap(transform(swap([(mid[3 * k + j, :, :INNER], mid[3 * k + j, :, INNER:]) for k in range(16)])))
        for i, s in enumerate(order):
            ret[c, s, 0, :, lanes(j)], ret[c, s, 1, :, lanes(j)] = out[i]


def local_terms(c, padded, base, coef, wave_ref):
    def body(i, carry):
        m, j = i // 3, i % 3
        lanes = pl.ds(pl.multiple_of(j * INNER, INNER), INNER)
        rate = TAU * 0.25 * wave_ref[m].astype(jnp.float32)
        for octet in range(ROWS // 8):
            rows = slice(8 * octet, 8 * octet + 8)
            sums = []
            for p in range(2):
                total = jnp.zeros((8, INNER), jnp.float32)
                for s in range(STEN):
                    total += coef[s, rows, :] * padded[m, c, p, 8 * octet + 1 + s : 8 * octet + 9 + s, lanes]
                sums.append(total)
            here = slice(8 * octet + 8, 8 * octet + 16)
            re, im = padded[m, c, 0, here, lanes], padded[m, c, 1, here, lanes]
            turn = rate * coef[STEN, rows, :]
            sums[0] += re - turn * im
            sums[1] += im + turn * re
            if c == 1:
                couple = TAU * coef[STEN + 1, rows, :]
                for p in range(2):
                    sums[p] -= couple * padded[m, 0, p, here, lanes]
            for p in range(2):
                base[m, c, p, rows, lanes] = sums[p]
        return carry

    lax.fori_loop(0, MODES * 3, body, 0)


def kernel(
    field, mean_flow, d2_coef, wall_coef, kx_index, patch_of, pair_hbm, trig_hbm,
    base_out, spw, grad_out,
    padded, base, recv, ret, work, mid, pair, trig, coef, turned, flow, sten, wc, kx, patch, edge, grads, shares,
    load_sem, own_sem, back_sem, f_send, f_recv, r_send, r_recv, h_send, h_recv, s_send, s_recv, g_send, g_recv,
    out_sem, edge_sem,
):
    w, me = lax.axis_index("wall"), lax.axis_index("span")
    at_low, at_high = w == 0, w == WALLS - 1
    at_edge = jnp.logical_or(at_low, at_high)

    def span_of(offset, sign=1):
        hi = lax.rem(me // 8 + offset[0], 2)
        return hi * 8 + lax.rem(lax.rem(me, 8) + 8 + sign * offset[1], 8)

    loads = [
        pltpu.make_async_copy(field, padded.at[:, :, :, pl.ds(8, ROWS), :], load_sem.at[0]),
        pltpu.make_async_copy(mean_flow, flow, load_sem.at[1]),
        pltpu.make_async_copy(d2_coef, sten, load_sem.at[2]),
        pltpu.make_async_copy(wall_coef, wc, load_sem.at[3]),
        pltpu.make_async_copy(kx_index, kx, load_sem.at[4]),
        pltpu.make_async_copy(patch_of, patch.at[0], load_sem.at[5]),
        pltpu.make_async_copy(pair_hbm, pair, load_sem.at[6]),
        pltpu.make_async_copy(trig_hbm, trig, load_sem.at[7]),
    ]

    barrier = pltpu.get_barrier_semaphore()
    for offset in OFFSETS:
        pl.semaphore_signal(barrier, inc=1, device_id=(w, span_of(offset)), device_id_type=MESH)

    def greet(wall):
        pl.semaphore_signal(barrier, inc=1, device_id=(wall, me), device_id_type=MESH)

    pl.when(w > 0)(lambda: greet(w - 1))
    pl.when(w < WALLS - 1)(lambda: greet(w + 1))
    pl.when(w > 1)(lambda: greet(0))
    pl.when(w < WALLS - 2)(lambda: greet(WALLS - 1))
    for load in loads:
        load.start()
    pl.when(at_edge)(lambda: pl.semaphore_wait(barrier, SPANS - 1 + WALLS - 1))
    pl.when(jnp.logical_not(at_edge))(lambda: pl.semaphore_wait(barrier, SPANS - 1 + 2))

    def block(t, c):
        return (t // 4, c, slice(None), pl.ds(pl.multiple_of(8 * lax.rem(t, 4), 8), 8), slice(None))

    def forward(c, t, slot):
        return pltpu.make_async_remote_copy(
            src_ref=field.at[block(t, c)], dst_ref=recv.at[c, slot], send_sem=f_send.at[c, t],
            recv_sem=f_recv.at[c, slot], device_id=(w, t), device_id_type=MESH)

    def backward(c, t, slot):
        return pltpu.make_async_remote_copy(
            src_ref=ret.at[c, t], dst_ref=spw.at[block(slot, c)], send_sem=r_send.at[c, t],
            recv_sem=r_recv.at[c, slot], device_id=(w, t), device_id_type=MESH)

    def own(c):
        return pltpu.make_async_copy(field.at[block(me, c)], recv.at[c, me], own_sem.at[c])

    def own_back(c):
        return pltpu.make_async_copy(ret.at[c, me], spw.at[block(me, c)], back_sem.at[c])

    def send_lines(c):
        for offset in OFFSETS:
            forward(c, span_of(offset), me).start()
        own(c).start()

    def take_lines(c):
        for offset in OFFSETS:
            forward(c, me, span_of(offset, -1)).wait_recv()
        own(c).wait()

    def send_back(c):
        for offset in OFFSETS:
            backward(c, span_of(offset), me).start()
        own_back(c).start()

    def take_back(c):
        for offset in OFFSETS:
            backward(c, me, span_of(offset, -1)).wait_recv()
        own_back(c).wait()

    def halo(up):
        src = pl.ds(ROWS - 8 if up else 0, 8)
        dst = pl.ds(0 if up else ROWS + 8, 8)
        return pltpu.make_async_remote_copy(
            src_ref=field.at[:, :, :, src, :], dst_ref=padded.at[:, :, :, dst, :], send_sem=h_send.at[int(up)],
            recv_sem=h_recv.at[int(up)], device_id=(w + 1 if up else w - 1, me), device_id_type=MESH)

    send_lines(0)
    pl.when(w < WALLS - 1)(lambda: halo(True).start())
    pl.when(w > 0)(lambda: halo(False).start())
    send_lines(1)

    @pl.when(at_low)
    def _():
        padded[:, :, :, 0:8, :] = jnp.zeros((MODES, COMPS, 2, 8, COLS), jnp.float32)

    @pl.when(at_high)
    def _():
        padded[:, :, :, ROWS + 8 :, :] = jnp.zeros((MODES, COMPS, 2, 8, COLS), jnp.float32)

    for load in loads:
        load.wait()
    turned[...] = jnp.zeros((INNER, INNER), jnp.float32)
    turned[0:STEN, 0:ROWS] = sten[...]
    turned[STEN : STEN + 2, 0:ROWS] = flow[...]
    columns = turned[...].T
    for k in range(STEN + 2):
        coef[k] = jnp.broadcast_to(columns[0:ROWS, k : k + 1], (ROWS, INNER))

    pl.when(w > 0)(lambda: halo(True).wait_recv())
    pl.when(w < WALLS - 1)(lambda: halo(False).wait_recv())
    local_terms(0, padded, base, coef, kx)

    take_lines(0)
    filter_lines(0, recv, ret, work, mid, pair, trig)
    send_back(0)
    send_lines(2)

    local_terms(1, padded, base, coef, kx)
    take_lines(1)
    filter_lines(1, recv, ret, work, mid, pair, trig)

    def share(t, slot):
        return pltpu.make_async_remote_copy(
            src_ref=grads.at[2], dst_ref=shares.at[slot], send_sem=s_send.at[t], recv_sem=s_recv.at[slot],
            device_id=(w, t), device_id_type=MESH)

    take_back(0)

    @pl.when(at_edge)
    def _():
        rows = pl.ds(pl.multiple_of(jnp.where(at_low, 0, ROWS - 8), 8), 8)
        copy = pltpu.make_async_copy(spw.at[:, 0, :, rows, :], edge, edge_sem)
        copy.start()
        copy.wait()
        line = lax.broadcasted_iota(jnp.int32, (8, COLS), 0)
        weight = jnp.zeros((8, COLS), jnp.float32)
        for j in range(8):
            weight = jnp.where(line == j, jnp.where(at_low, wc[0, j], wc[1, 7 - j]), weight)
        patches = (lax.broadcasted_iota(jnp.int32, (INNER, COLS), 0) == patch[...]).astype(jnp.bfloat16)
        sums = []
        for m in range(MODES):
            for p in range(2):
                values = weight * (base[m, 0, p, rows, :] + edge[m, p])
                sums.append(jnp.sum(values, axis=0, keepdims=True))
        rest = jnp.concatenate(sums, axis=0)
        total = jnp.zeros((8, INNER), jnp.float32)
        for _ in range(3):
            part = rest.astype(jnp.bfloat16)
            rest = rest - part.astype(jnp.float32)
            total += lax.dot_general(part, patches, (((1,), (1,)), ((), ())), preferred_element_type=jnp.float32)
        grads[2] = total
        for offset in OFFSETS:
            share(span_of(offset), me).start()

    send_back(1)
    local_terms(2, padded, base, coef, kx)
    base_copy = pltpu.make_async_copy(base, base_out, out_sem.at[0])
    base_copy.start()
    take_lines(2)
    filter_lines(2, recv, ret, work, mid, pair, trig)

    def spread(side, t):
        return pltpu.make_async_remote_copy(
            src_ref=grads.at[side], dst_ref=grads.at[side], send_sem=g_send.at[t], recv_sem=g_recv.at[side],
            device_id=(t, me), device_id_type=MESH)

    @pl.when(at_edge)
    def _():
        for offset in OFFSETS:
            share(me, span_of(offset, -1)).wait_recv()
        shares[me] = grads[2]
        total = shares[0]
        for s in range(1, SPANS):
            total += shares[s]
        grads[jnp.where(at_low, 0, 1)] = total

    @pl.when(at_low)
    def _():
        for t in range(1, WALLS):
            spread(0, t).start()

    @pl.when(at_high)
    def _():
        for t in range(WALLS - 1):
            spread(1, t).start()

    send_back(2)
    take_back(1)
    pl.when(jnp.logical_not(at_low))(lambda: spread(0, w).wait_recv())
    pl.when(jnp.logical_not(at_high))(lambda: spread(1, w).wait_recv())
    grad_copy = pltpu.make_async_copy(grads.at[pl.ds(0, 2)], grad_out, out_sem.at[1])
    grad_copy.start()
    take_back(2)
    for c in range(COMPS):
        for offset in OFFSETS:
            forward(c, span_of(offset), me).wait_send()
            backward(c, span_of(offset), me).wait_send()
    pl.when(w < WALLS - 1)(lambda: halo(True).wait_send())
    pl.when(w > 0)(lambda: halo(False).wait_send())

    @pl.when(at_edge)
    def _():
        for offset in OFFSETS:
            share(span_of(offset), me).wait_send()

    @pl.when(at_low)
    def _():
        for t in range(1, WALLS):
            spread(0, t).wait_send()

    @pl.when(at_high)
    def _():
        for t in range(WALLS - 1):
            spread(1, t).wait_send()

    base_copy.wait()
    grad_copy.wait()


def on_device(field, mean_flow, d2_coef, wall_coef, kx_index, patch_of):
    pair, trig = tables()
    arrays = (field, mean_flow, d2_coef, wall_coef, kx_index, patch_of, pair, trig)
    whole = (MODES, COMPS, 2, ROWS, COLS)
    dma = pltpu.SemaphoreType.DMA
    base, spanwise, grads = pl.pallas_call(
        kernel,
        out_shape=[
            jax.ShapeDtypeStruct(whole, jnp.float32),
            jax.ShapeDtypeStruct(whole, jnp.float32),
            jax.ShapeDtypeStruct((2, 8, INNER), jnp.float32),
        ],
        in_specs=[pl.BlockSpec(memory_space=pl.ANY)] * 8,
        out_specs=[pl.BlockSpec(memory_space=pl.ANY)] * 3,
        scratch_shapes=[
            pltpu.VMEM((MODES, COMPS, 2, ROWS + 16, COLS), jnp.float32),
            pltpu.VMEM(whole, jnp.float32),
            pltpu.VMEM((COMPS, SPANS, 2, 8, COLS), jnp.float32),
            pltpu.VMEM((COMPS, SPANS, 2, 8, COLS), jnp.float32),
            pltpu.VMEM((OUTER, 8, 2 * INNER), jnp.float32),
            pltpu.VMEM((OUTER, 8, 2 * INNER), jnp.float32),
            pltpu.VMEM((2, 2, 2 * INNER, 2 * INNER), jnp.bfloat16),
            pltpu.VMEM((OUTER, 3, INNER), jnp.float32),
            pltpu.VMEM((STEN + 2, ROWS, INNER), jnp.float32),
            pltpu.VMEM((INNER, INNER), jnp.float32),
            pltpu.VMEM((2, ROWS), jnp.float32),
            pltpu.VMEM((STEN, ROWS), jnp.float32),
            pltpu.SMEM((2, 8), jnp.float32),
            pltpu.SMEM((MODES,), jnp.int32),
            pltpu.VMEM((1, COLS), jnp.int32),
            pltpu.VMEM((MODES, 2, 8, COLS), jnp.float32),
            pltpu.VMEM((3, 8, INNER), jnp.float32),
            pltpu.VMEM((SPANS, 8, INNER), jnp.float32),
            dma((8,)),
            dma((COMPS,)),
            dma((COMPS,)),
            dma((COMPS, SPANS)),
            dma((COMPS, SPANS)),
            dma((COMPS, SPANS)),
            dma((COMPS, SPANS)),
            dma((2,)),
            dma((2,)),
            dma((SPANS,)),
            dma((SPANS,)),
            dma((WALLS,)),
            dma((2,)),
            dma((2,)),
            dma,
        ],
        compiler_params=pltpu.CompilerParams(collective_id=0, has_side_effects=True, vmem_limit_bytes=16 * 2**20),
    )(*[pltpu.with_memory_space_constraint(jnp.asarray(array), pltpu.HBM) for array in arrays])
    new_field = base + spanwise
    wall_grad = grads[:, :, :PATCH].reshape(2, MODES, 2, PATCH)
    return new_field, wall_grad


def solution(mesh):
    return jax.shard_map(
        on_device,
        mesh=mesh,
        in_specs=(
            P(None, None, None, "wall", "span"),
            P(None, "wall"),
            P(None, "wall"),
            P(),
            P(),
            P("span"),
        ),
        out_specs=(P(None, None, None, "wall", "span"), P()),
        check_vma=False,
    )
```

```python
import math

import jax
import jax.numpy as jnp
import numpy as np
from jax import lax
from jax.experimental import pallas as pl
from jax.experimental.pallas import tpu as pltpu
from jax.sharding import PartitionSpec as P

MESH = pl.DeviceIdType.MESH
MODES, COMPS, ROWS, COLS = 4, 3, 32, 384
WALLS, SPANS = 16, 16
STEN = 15
PATCH = 64
NZ = SPANS * COLS
INNER = 128
OUTER = NZ // INNER
CUTOFF = NZ // 3
VIS = 0.5
TAU = 0.25

OFFSETS = sorted(
    [(hi, z) for hi in range(2) for z in range(8) if hi or z],
    key=lambda o: (2 * o[0] + min(o[1], 8 - o[1]), o),
)


def tables():
    outer = np.array([next(k for k in range(OUTER) if k % 16 == i // 3 and k % 3 == i % 3) for i in range(OUTER)])
    inner = np.arange(INNER)
    angle = 2.0 * np.pi * (outer[:, None] * inner[None, :] % NZ) / NZ
    twist = np.stack([np.cos(angle), np.sin(angle)], axis=1)
    wave = outer[:, None] + OUTER * inner[None, :]
    signed = np.where(wave > NZ // 2, wave - NZ, wave)
    factor = np.where(np.abs(signed) < CUTOFF, -VIS * (signed / CUTOFF) ** 2, 0.0) / NZ
    angle = 2.0 * np.pi * (inner[:, None] * inner[None, :] % INNER) / INNER
    c, s = np.cos(angle), np.sin(angle)
    pair = []
    for table in (np.block([[c, -s], [s, c]]), np.block([[c, s], [-s, c]])):
        high = table.astype(np.float32).astype(jnp.bfloat16)
        low = (table - high.astype(np.float64)).astype(np.float32).astype(jnp.bfloat16)
        pair.append(np.stack([high, low]))
    rows = np.concatenate([twist, factor[:, None]], axis=1).astype(np.float32)
    return np.stack(pair), rows


def times(value, cos, sin):
    re, im = value
    half = math.sqrt(0.5)
    if abs(sin) < 1e-12:
        return (re, im) if cos > 0 else (-re, -im)
    if abs(cos) < 1e-12:
        return (im, -re) if sin > 0 else (-im, re)
    if abs(abs(cos) - half) < 1e-12 and abs(abs(sin) - half) < 1e-12:
        a, b = math.copysign(half, cos), math.copysign(half, sin)
        if a == b:
            return ((re + im) * a, (im - re) * a)
        return ((re - im) * a, (im + re) * a)
    return (re * cos + im * sin, im * cos - re * sin)


def transform(values):
    n = len(values)
    if n == 1:
        return values
    even, odd = transform(values[0::2]), transform(values[1::2])
    first, second = [], []
    for k in range(n // 2):
        a = 2.0 * math.pi * k / n
        t = times(odd[k], math.cos(a), math.sin(a))
        first.append((even[k][0] + t[0], even[k][1] + t[1]))
        second.append((even[k][0] - t[0], even[k][1] - t[1]))
    return first + second


def transform_three(x):
    (ar, ai), (br, bi), (cr, ci) = x
    sr, si, dr, di = br + cr, bi + ci, br - cr, bi - ci
    mr, mi = ar - 0.5 * sr, ai - 0.5 * si
    h = math.sqrt(0.75)
    return [(ar + sr, ai + si), (mr + h * di, mi - h * dr), (mr - h * di, mi + h * dr)]


def swap(values):
    return [(im, re) for re, im in values]


def multiply(values, pair_ref, which):
    high = values.astype(jnp.bfloat16)
    low = (values - high.astype(jnp.float32)).astype(jnp.bfloat16)
    out = jnp.dot(high, pair_ref[which, 0], preferred_element_type=jnp.float32)
    out += jnp.dot(low, pair_ref[which, 0], preferred_element_type=jnp.float32)
    out += jnp.dot(high, pair_ref[which, 1], preferred_element_type=jnp.float32)
    return out


def filter_lines(c, recv, ret, work, mid, pair, trig):
    def lanes(j):
        return slice(INNER * j, INNER * (j + 1))

    for j in range(3):
        order = [(i + 5 * j) % 16 for i in range(16)]
        out = transform([(recv[c, s, 0, :, lanes(j)], recv[c, s, 1, :, lanes(j)]) for s in order])
        for k in range(16):
            work[3 * k + j, :, :INNER], work[3 * k + j, :, INNER:] = out[k]
    for k in range(16):
        out = transform_three([(work[3 * k + j, :, :INNER], work[3 * k + j, :, INNER:]) for j in range(3)])
        for i, (re, im) in enumerate(out):
            cos, sin = trig[3 * k + i, 0:1, :], trig[3 * k + i, 1:2, :]
            mid[3 * k + i, :, :INNER] = re * cos + im * sin
            mid[3 * k + i, :, INNER:] = im * cos - re * sin
    modes = multiply(mid[...].reshape(OUTER * 8, 2 * INNER), pair, 0).reshape(OUTER, 8, 2 * INNER)
    work[...] = modes
    for k in range(OUTER):
        factor = trig[k, 2:3, :]
        mid[k, :, :INNER] = work[k, :, :INNER] * factor
        mid[k, :, INNER:] = work[k, :, INNER:] * factor
    work[...] = multiply(mid[...].reshape(OUTER * 8, 2 * INNER), pair, 1).reshape(OUTER, 8, 2 * INNER)
    for k in range(16):
        values = []
        for i in range(3):
            re, im = work[3 * k + i, :, :INNER], work[3 * k + i, :, INNER:]
            cos, sin = trig[3 * k + i, 0:1, :], trig[3 * k + i, 1:2, :]
            values.append((re * cos - im * sin, im * cos + re * sin))
        out = swap(transform_three(swap(values)))
        for j in range(3):
            mid[3 * k + j, :, :INNER], mid[3 * k + j, :, INNER:] = out[j]
    for j in range(3):
        order = [(i + 5 * j) % 16 for i in range(16)]
        out = swap(transform(swap([(mid[3 * k + j, :, :INNER], mid[3 * k + j, :, INNER:]) for k in range(16)])))
        for i, s in enumerate(order):
            ret[c, s, 0, :, lanes(j)], ret[c, s, 1, :, lanes(j)] = out[i]


def local_terms(c, padded, base, coef, wave_ref):
    def body(i, carry):
        m, j = i // 3, i % 3
        lanes = pl.ds(pl.multiple_of(j * INNER, INNER), INNER)
        rate = TAU * 0.25 * wave_ref[m].astype(jnp.float32)
        for octet in range(ROWS // 8):
            rows = slice(8 * octet, 8 * octet + 8)
            sums = []
            for p in range(2):
                total = jnp.zeros((8, INNER), jnp.float32)
                for s in range(STEN):
                    total += coef[s, rows, :] * padded[m, c, p, 8 * octet + 1 + s : 8 * octet + 9 + s, lanes]
                sums.append(total)
            here = slice(8 * octet + 8, 8 * octet + 16)
            re, im = padded[m, c, 0, here, lanes], padded[m, c, 1, here, lanes]
            turn = rate * coef[STEN, rows, :]
            sums[0] += re - turn * im
            sums[1] += im + turn * re
            if c == 1:
                couple = TAU * coef[STEN + 1, rows, :]
                for p in range(2):
                    sums[p] -= couple * padded[m, 0, p, here, lanes]
            for p in range(2):
                base[m, c, p, rows, lanes] = sums[p]
        return carry

    lax.fori_loop(0, MODES * 3, body, 0)


def kernel(
    field, mean_flow, d2_coef, wall_coef, kx_index, patch_of, pair_hbm, trig_hbm,
    base_out, spw, grad_out,
    padded, base, recv, ret, work, mid, pair, trig, coef, turned, flow, sten, wc, kx, patch, edge, grads, shares,
    load_sem, f_send, f_recv, r_send, r_recv, h_send, h_recv, s_send, s_recv, g_send, g_recv,
    out_sem, edge_sem,
):
    w, me = lax.axis_index("wall"), lax.axis_index("span")
    at_low, at_high = w == 0, w == WALLS - 1
    at_edge = jnp.logical_or(at_low, at_high)

    def span_of(offset, sign=1):
        hi = lax.rem(me // 8 + offset[0], 2)
        return hi * 8 + lax.rem(lax.rem(me, 8) + 8 + sign * offset[1], 8)

    loads = [
        pltpu.make_async_copy(field, padded.at[:, :, :, pl.ds(8, ROWS), :], load_sem.at[0]),
        pltpu.make_async_copy(mean_flow, flow, load_sem.at[1]),
        pltpu.make_async_copy(d2_coef, sten, load_sem.at[2]),
        pltpu.make_async_copy(wall_coef, wc, load_sem.at[3]),
        pltpu.make_async_copy(kx_index, kx, load_sem.at[4]),
        pltpu.make_async_copy(patch_of, patch.at[0], load_sem.at[5]),
        pltpu.make_async_copy(pair_hbm, pair, load_sem.at[6]),
        pltpu.make_async_copy(trig_hbm, trig, load_sem.at[7]),
    ]

    barrier = pltpu.get_barrier_semaphore()
    for offset in OFFSETS:
        pl.semaphore_signal(barrier, inc=1, device_id=(w, span_of(offset)), device_id_type=MESH)

    def greet(wall):
        pl.semaphore_signal(barrier, inc=1, device_id=(wall, me), device_id_type=MESH)

    pl.when(w > 0)(lambda: greet(w - 1))
    pl.when(w < WALLS - 1)(lambda: greet(w + 1))
    pl.when(w > 1)(lambda: greet(0))
    pl.when(w < WALLS - 2)(lambda: greet(WALLS - 1))
    for load in loads:
        load.start()
    pl.when(at_edge)(lambda: pl.semaphore_wait(barrier, SPANS - 1 + WALLS - 1))
    pl.when(jnp.logical_not(at_edge))(lambda: pl.semaphore_wait(barrier, SPANS - 1 + 2))

    def block(t, c):
        return (t // 4, c, slice(None), pl.ds(pl.multiple_of(8 * lax.rem(t, 4), 8), 8), slice(None))

    def forward(c, t, slot):
        return pltpu.make_async_remote_copy(
            src_ref=field.at[block(t, c)], dst_ref=recv.at[c, slot], send_sem=f_send,
            recv_sem=f_recv.at[c], device_id=(w, t), device_id_type=MESH)

    def backward(c, t, slot):
        return pltpu.make_async_remote_copy(
            src_ref=ret.at[c, t], dst_ref=spw.at[block(slot, c)], send_sem=r_send,
            recv_sem=r_recv.at[c], device_id=(w, t), device_id_type=MESH)

    def wait_bytes(ref, sem):
        pltpu.make_async_copy(ref, ref, sem).wait()

    def own(c):
        return pltpu.make_async_copy(field.at[block(me, c)], recv.at[c, me], f_recv.at[c])

    def own_back(c):
        return pltpu.make_async_copy(ret.at[c, me], spw.at[block(me, c)], r_recv.at[c])

    def send_lines(c):
        for offset in OFFSETS:
            forward(c, span_of(offset), me).start()
        own(c).start()

    def take_lines(c):
        wait_bytes(recv.at[c], f_recv.at[c])

    def send_back(c):
        for offset in OFFSETS:
            backward(c, span_of(offset), me).start()
        own_back(c).start()

    def take_back(c):
        wait_bytes(spw.at[:, c], r_recv.at[c])

    def halo(up):
        src = pl.ds(ROWS - 8 if up else 0, 8)
        dst = pl.ds(0 if up else ROWS + 8, 8)
        return pltpu.make_async_remote_copy(
            src_ref=field.at[:, :, :, src, :], dst_ref=padded.at[:, :, :, dst, :], send_sem=h_send.at[int(up)],
            recv_sem=h_recv.at[int(up)], device_id=(w + 1 if up else w - 1, me), device_id_type=MESH)

    send_lines(0)
    pl.when(w < WALLS - 1)(lambda: halo(True).start())
    pl.when(w > 0)(lambda: halo(False).start())
    send_lines(1)

    @pl.when(at_low)
    def _():
        padded[:, :, :, 0:8, :] = jnp.zeros((MODES, COMPS, 2, 8, COLS), jnp.float32)

    @pl.when(at_high)
    def _():
        padded[:, :, :, ROWS + 8 :, :] = jnp.zeros((MODES, COMPS, 2, 8, COLS), jnp.float32)

    for load in loads:
        load.wait()
    turned[...] = jnp.zeros((INNER, INNER), jnp.float32)
    turned[0:STEN, 0:ROWS] = sten[...]
    turned[STEN : STEN + 2, 0:ROWS] = flow[...]
    columns = turned[...].T
    for k in range(STEN + 2):
        coef[k] = jnp.broadcast_to(columns[0:ROWS, k : k + 1], (ROWS, INNER))

    pl.when(w > 0)(lambda: halo(True).wait_recv())
    pl.when(w < WALLS - 1)(lambda: halo(False).wait_recv())
    local_terms(0, padded, base, coef, kx)

    take_lines(0)
    filter_lines(0, recv, ret, work, mid, pair, trig)
    send_back(0)
    send_lines(2)

    local_terms(1, padded, base, coef, kx)
    take_lines(1)
    filter_lines(1, recv, ret, work, mid, pair, trig)

    def share(t, slot):
        return pltpu.make_async_remote_copy(
            src_ref=grads.at[2], dst_ref=shares.at[slot], send_sem=s_send, recv_sem=s_recv,
            device_id=(w, t), device_id_type=MESH)

    take_back(0)

    @pl.when(at_edge)
    def _():
        rows = pl.ds(pl.multiple_of(jnp.where(at_low, 0, ROWS - 8), 8), 8)
        copy = pltpu.make_async_copy(spw.at[:, 0, :, rows, :], edge, edge_sem)
        copy.start()
        copy.wait()
        line = lax.broadcasted_iota(jnp.int32, (8, COLS), 0)
        weight = jnp.zeros((8, COLS), jnp.float32)
        for j in range(8):
            weight = jnp.where(line == j, jnp.where(at_low, wc[0, j], wc[1, 7 - j]), weight)
        patches = (lax.broadcasted_iota(jnp.int32, (INNER, COLS), 0) == patch[...]).astype(jnp.bfloat16)
        sums = []
        for m in range(MODES):
            for p in range(2):
                values = weight * (base[m, 0, p, rows, :] + edge[m, p])
                sums.append(jnp.sum(values, axis=0, keepdims=True))
        rest = jnp.concatenate(sums, axis=0)
        total = jnp.zeros((8, INNER), jnp.float32)
        for _ in range(3):
            part = rest.astype(jnp.bfloat16)
            rest = rest - part.astype(jnp.float32)
            total += lax.dot_general(part, patches, (((1,), (1,)), ((), ())), preferred_element_type=jnp.float32)
        grads[2] = total
        for offset in OFFSETS:
            share(span_of(offset), me).start()

    send_back(1)
    local_terms(2, padded, base, coef, kx)
    base_copy = pltpu.make_async_copy(base, base_out, out_sem.at[0])
    base_copy.start()
    take_lines(2)
    filter_lines(2, recv, ret, work, mid, pair, trig)

    def spread(side, t):
        return pltpu.make_async_remote_copy(
            src_ref=grads.at[side], dst_ref=grads.at[side], send_sem=g_send, recv_sem=g_recv.at[side],
            device_id=(t, me), device_id_type=MESH)

    @pl.when(at_edge)
    def _():
        wait_bytes(shares.at[pl.ds(0, SPANS - 1)], s_recv)
        shares[me] = grads[2]
        total = shares[0]
        for s in range(1, SPANS):
            total += shares[s]
        grads[jnp.where(at_low, 0, 1)] = total

    @pl.when(at_low)
    def _():
        for t in range(1, WALLS):
            spread(0, t).start()

    @pl.when(at_high)
    def _():
        for t in range(WALLS - 1):
            spread(1, t).start()

    send_back(2)
    take_back(1)
    pl.when(jnp.logical_not(at_low))(lambda: spread(0, w).wait_recv())
    pl.when(jnp.logical_not(at_high))(lambda: spread(1, w).wait_recv())
    grad_copy = pltpu.make_async_copy(grads.at[pl.ds(0, 2)], grad_out, out_sem.at[1])
    grad_copy.start()

    wait_bytes(recv.at[:, pl.ds(0, SPANS - 1)], f_send)
    pl.when(w < WALLS - 1)(lambda: halo(True).wait_send())
    pl.when(w > 0)(lambda: halo(False).wait_send())

    @pl.when(at_edge)
    def _():
        wait_bytes(shares.at[pl.ds(0, SPANS - 1)], s_send)

        wait_bytes(shares.at[pl.ds(0, WALLS - 1)], g_send)

    base_copy.wait()
    grad_copy.wait()
    wait_bytes(ret.at[:, pl.ds(0, SPANS - 1)], r_send)
    take_back(2)


def on_device(field, mean_flow, d2_coef, wall_coef, kx_index, patch_of):
    pair, trig = tables()
    arrays = (field, mean_flow, d2_coef, wall_coef, kx_index, patch_of, pair, trig)
    whole = (MODES, COMPS, 2, ROWS, COLS)
    dma = pltpu.SemaphoreType.DMA
    base, spanwise, grads = pl.pallas_call(
        kernel,
        out_shape=[
            jax.ShapeDtypeStruct(whole, jnp.float32),
            jax.ShapeDtypeStruct(whole, jnp.float32),
            jax.ShapeDtypeStruct((2, 8, INNER), jnp.float32),
        ],
        in_specs=[pl.BlockSpec(memory_space=pl.ANY)] * 8,
        out_specs=[pl.BlockSpec(memory_space=pl.ANY)] * 3,
        scratch_shapes=[
            pltpu.VMEM((MODES, COMPS, 2, ROWS + 16, COLS), jnp.float32),
            pltpu.VMEM(whole, jnp.float32),
            pltpu.VMEM((COMPS, SPANS, 2, 8, COLS), jnp.float32),
            pltpu.VMEM((COMPS, SPANS, 2, 8, COLS), jnp.float32),
            pltpu.VMEM((OUTER, 8, 2 * INNER), jnp.float32),
            pltpu.VMEM((OUTER, 8, 2 * INNER), jnp.float32),
            pltpu.VMEM((2, 2, 2 * INNER, 2 * INNER), jnp.bfloat16),
            pltpu.VMEM((OUTER, 3, INNER), jnp.float32),
            pltpu.VMEM((STEN + 2, ROWS, INNER), jnp.float32),
            pltpu.VMEM((INNER, INNER), jnp.float32),
            pltpu.VMEM((2, ROWS), jnp.float32),
            pltpu.VMEM((STEN, ROWS), jnp.float32),
            pltpu.SMEM((2, 8), jnp.float32),
            pltpu.SMEM((MODES,), jnp.int32),
            pltpu.VMEM((1, COLS), jnp.int32),
            pltpu.VMEM((MODES, 2, 8, COLS), jnp.float32),
            pltpu.VMEM((3, 8, INNER), jnp.float32),
            pltpu.VMEM((SPANS, 8, INNER), jnp.float32),
            dma((8,)),
            dma,
            dma((COMPS,)),
            dma,
            dma((COMPS,)),
            dma((2,)),
            dma((2,)),
            dma,
            dma,
            dma,
            dma((2,)),
            dma((2,)),
            dma,
        ],
        compiler_params=pltpu.CompilerParams(collective_id=0, has_side_effects=True, vmem_limit_bytes=16 * 2**20),
    )(*[pltpu.with_memory_space_constraint(jnp.asarray(array), pltpu.HBM) for array in arrays])
    new_field = base + spanwise
    wall_grad = grads[:, :, :PATCH].reshape(2, MODES, 2, PATCH)
    return new_field, wall_grad


def solution(mesh):
    return jax.shard_map(
        on_device,
        mesh=mesh,
        in_specs=(
            P(None, None, None, "wall", "span"),
            P(None, "wall"),
            P(None, "wall"),
            P(),
            P(),
            P("span"),
        ),
        out_specs=(P(None, None, None, "wall", "span"), P()),
        check_vma=False,
    )
```

```python
import math

import jax
import jax.numpy as jnp
import numpy as np
from jax import lax
from jax.experimental import pallas as pl
from jax.experimental.pallas import tpu as pltpu
from jax.sharding import PartitionSpec as P

MESH = pl.DeviceIdType.MESH
MODES, COMPS, ROWS, COLS = 4, 3, 32, 384
WALLS, SPANS = 16, 16
STEN = 15
PATCH = 64
NZ = SPANS * COLS
INNER = 128
OUTER = NZ // INNER
CUTOFF = NZ // 3
VIS = 0.5
TAU = 0.25

OFFSETS = sorted(
    [(hi, z) for hi in range(2) for z in range(8) if hi or z],
    key=lambda o: (2 * o[0] + min(o[1], 8 - o[1]), o),
)


def tables():
    outer = np.array([next(k for k in range(OUTER) if k % 16 == i // 3 and k % 3 == i % 3) for i in range(OUTER)])
    inner = np.arange(INNER)
    angle = 2.0 * np.pi * (outer[:, None] * inner[None, :] % NZ) / NZ
    twist = np.stack([np.cos(angle), np.sin(angle)], axis=1)
    wave = outer[:, None] + OUTER * inner[None, :]
    signed = np.where(wave > NZ // 2, wave - NZ, wave)
    factor = np.where(np.abs(signed) < CUTOFF, -VIS * (signed / CUTOFF) ** 2, 0.0) / NZ
    angle = 2.0 * np.pi * (inner[:, None] * inner[None, :] % INNER) / INNER
    c, s = np.cos(angle), np.sin(angle)
    pair = []
    for table in (np.block([[c, -s], [s, c]]), np.block([[c, s], [-s, c]])):
        high = table.astype(np.float32).astype(jnp.bfloat16)
        low = (table - high.astype(np.float64)).astype(np.float32).astype(jnp.bfloat16)
        pair.append(np.stack([high, low]))
    rows = np.concatenate([twist, factor[:, None]], axis=1).astype(np.float32)
    return np.stack(pair), rows


def times(value, cos, sin):
    re, im = value
    half = math.sqrt(0.5)
    if abs(sin) < 1e-12:
        return (re, im) if cos > 0 else (-re, -im)
    if abs(cos) < 1e-12:
        return (im, -re) if sin > 0 else (-im, re)
    if abs(abs(cos) - half) < 1e-12 and abs(abs(sin) - half) < 1e-12:
        a, b = math.copysign(half, cos), math.copysign(half, sin)
        if a == b:
            return ((re + im) * a, (im - re) * a)
        return ((re - im) * a, (im + re) * a)
    return (re * cos + im * sin, im * cos - re * sin)


def transform(values):
    n = len(values)
    if n == 1:
        return values
    even, odd = transform(values[0::2]), transform(values[1::2])
    first, second = [], []
    for k in range(n // 2):
        a = 2.0 * math.pi * k / n
        t = times(odd[k], math.cos(a), math.sin(a))
        first.append((even[k][0] + t[0], even[k][1] + t[1]))
        second.append((even[k][0] - t[0], even[k][1] - t[1]))
    return first + second


def transform_three(x):
    (ar, ai), (br, bi), (cr, ci) = x
    sr, si, dr, di = br + cr, bi + ci, br - cr, bi - ci
    mr, mi = ar - 0.5 * sr, ai - 0.5 * si
    h = math.sqrt(0.75)
    return [(ar + sr, ai + si), (mr + h * di, mi - h * dr), (mr - h * di, mi + h * dr)]


def swap(values):
    return [(im, re) for re, im in values]


def multiply(values, pair_ref, which):
    high = values.astype(jnp.bfloat16)
    low = (values - high.astype(jnp.float32)).astype(jnp.bfloat16)
    out = jnp.dot(high, pair_ref[which, 0], preferred_element_type=jnp.float32)
    out += jnp.dot(low, pair_ref[which, 0], preferred_element_type=jnp.float32)
    out += jnp.dot(high, pair_ref[which, 1], preferred_element_type=jnp.float32)
    return out


def filter_lines(c, recv, ret, work, mid, pair, trig):
    def lanes(j):
        return slice(INNER * j, INNER * (j + 1))

    for j in range(3):
        order = [(i + 5 * j) % 16 for i in range(16)]
        out = transform([(recv[c, s, 0, :, lanes(j)], recv[c, s, 1, :, lanes(j)]) for s in order])
        for k in range(16):
            work[3 * k + j, :, :INNER], work[3 * k + j, :, INNER:] = out[k]
    for k in range(16):
        out = transform_three([(work[3 * k + j, :, :INNER], work[3 * k + j, :, INNER:]) for j in range(3)])
        for i, (re, im) in enumerate(out):
            cos, sin = trig[3 * k + i, 0:1, :], trig[3 * k + i, 1:2, :]
            mid[3 * k + i, :, :INNER] = re * cos + im * sin
            mid[3 * k + i, :, INNER:] = im * cos - re * sin
    modes = multiply(mid[...].reshape(OUTER * 8, 2 * INNER), pair, 0).reshape(OUTER, 8, 2 * INNER)
    work[...] = modes
    for k in range(OUTER):
        factor = trig[k, 2:3, :]
        mid[k, :, :INNER] = work[k, :, :INNER] * factor
        mid[k, :, INNER:] = work[k, :, INNER:] * factor
    work[...] = multiply(mid[...].reshape(OUTER * 8, 2 * INNER), pair, 1).reshape(OUTER, 8, 2 * INNER)
    for k in range(16):
        values = []
        for i in range(3):
            re, im = work[3 * k + i, :, :INNER], work[3 * k + i, :, INNER:]
            cos, sin = trig[3 * k + i, 0:1, :], trig[3 * k + i, 1:2, :]
            values.append((re * cos - im * sin, im * cos + re * sin))
        out = swap(transform_three(swap(values)))
        for j in range(3):
            mid[3 * k + j, :, :INNER], mid[3 * k + j, :, INNER:] = out[j]
    for j in range(3):
        order = [(i + 5 * j) % 16 for i in range(16)]
        out = swap(transform(swap([(mid[3 * k + j, :, :INNER], mid[3 * k + j, :, INNER:]) for k in range(16)])))
        for i, s in enumerate(order):
            ret[c, s, 0, :, lanes(j)], ret[c, s, 1, :, lanes(j)] = out[i]


def local_terms(c, padded, base, coef, wave_ref):
    def body(i, carry):
        m, j = i // 3, i % 3
        lanes = pl.ds(pl.multiple_of(j * INNER, INNER), INNER)
        rate = TAU * 0.25 * wave_ref[m].astype(jnp.float32)
        for octet in range(ROWS // 8):
            rows = slice(8 * octet, 8 * octet + 8)
            sums = []
            for p in range(2):
                total = jnp.zeros((8, INNER), jnp.float32)
                for s in range(STEN):
                    total += coef[s, rows, :] * padded[m, c, p, 8 * octet + 1 + s : 8 * octet + 9 + s, lanes]
                sums.append(total)
            here = slice(8 * octet + 8, 8 * octet + 16)
            re, im = padded[m, c, 0, here, lanes], padded[m, c, 1, here, lanes]
            turn = rate * coef[STEN, rows, :]
            sums[0] += re - turn * im
            sums[1] += im + turn * re
            if c == 1:
                couple = TAU * coef[STEN + 1, rows, :]
                for p in range(2):
                    sums[p] -= couple * padded[m, 0, p, here, lanes]
            for p in range(2):
                base[m, c, p, rows, lanes] = sums[p]
        return carry

    lax.fori_loop(0, MODES * 3, body, 0)


def kernel(
    field, mean_flow, d2_coef, wall_coef, kx_index, patch_of, pair_hbm, trig_hbm,
    base_out, spw, grad_out,
    padded, base, recv, ret, work, mid, pair, trig, coef, turned, flow, sten, wc, kx, patch, edge, grads, shares,
    load_sem, f_send, f_recv, r_send, r_recv, h_send, h_recv, s_send, s_recv, g_send, g_recv,
    out_sem, edge_sem,
):
    w, me = lax.axis_index("wall"), lax.axis_index("span")
    at_low, at_high = w == 0, w == WALLS - 1
    at_edge = jnp.logical_or(at_low, at_high)

    def span_of(offset, sign=1):
        hi = lax.rem(me // 8 + offset[0], 2)
        return hi * 8 + lax.rem(lax.rem(me, 8) + 8 + sign * offset[1], 8)

    loads = [
        pltpu.make_async_copy(field, padded.at[:, :, :, pl.ds(8, ROWS), :], load_sem.at[0]),
        pltpu.make_async_copy(mean_flow, flow, load_sem.at[1]),
        pltpu.make_async_copy(d2_coef, sten, load_sem.at[2]),
        pltpu.make_async_copy(wall_coef, wc, load_sem.at[3]),
        pltpu.make_async_copy(kx_index, kx, load_sem.at[4]),
        pltpu.make_async_copy(patch_of, patch.at[0], load_sem.at[5]),
        pltpu.make_async_copy(pair_hbm, pair, load_sem.at[6]),
        pltpu.make_async_copy(trig_hbm, trig, load_sem.at[7]),
    ]

    barrier = pltpu.get_barrier_semaphore()
    for offset in OFFSETS:
        pl.semaphore_signal(barrier, inc=1, device_id=(w, span_of(offset)), device_id_type=MESH)

    def greet(wall):
        pl.semaphore_signal(barrier, inc=1, device_id=(wall, me), device_id_type=MESH)

    pl.when(w > 0)(lambda: greet(w - 1))
    pl.when(w < WALLS - 1)(lambda: greet(w + 1))
    pl.when(w > 1)(lambda: greet(0))
    pl.when(w < WALLS - 2)(lambda: greet(WALLS - 1))
    for load in loads:
        load.start()
    pl.when(at_edge)(lambda: pl.semaphore_wait(barrier, SPANS - 1 + WALLS - 1))
    pl.when(jnp.logical_not(at_edge))(lambda: pl.semaphore_wait(barrier, SPANS - 1 + 2))

    def block(t, c):
        return (t // 4, c, slice(None), pl.ds(pl.multiple_of(8 * lax.rem(t, 4), 8), 8), slice(None))

    def forward(c, t, slot):
        return pltpu.make_async_remote_copy(
            src_ref=field.at[block(t, c)], dst_ref=recv.at[c, slot], send_sem=f_send,
            recv_sem=f_recv.at[c], device_id=(w, t), device_id_type=MESH)

    def backward(c, t, slot):
        return pltpu.make_async_remote_copy(
            src_ref=ret.at[c, t], dst_ref=spw.at[block(slot, c)], send_sem=r_send,
            recv_sem=r_recv.at[c], device_id=(w, t), device_id_type=MESH)

    def wait_bytes(ref, sem):
        pltpu.make_async_copy(ref, ref, sem).wait()

    def own(c):
        return pltpu.make_async_copy(field.at[block(me, c)], recv.at[c, me], f_recv.at[c])

    def own_back(c):
        return pltpu.make_async_copy(ret.at[c, me], spw.at[block(me, c)], r_recv.at[c])

    def send_lines(c):
        for offset in OFFSETS:
            forward(c, span_of(offset), me).start()
        own(c).start()

    def take_lines(c):
        wait_bytes(recv.at[c], f_recv.at[c])

    def send_back(c):
        for offset in OFFSETS:
            backward(c, span_of(offset), me).start()
        own_back(c).start()

    def take_back(c):
        wait_bytes(spw.at[:, c], r_recv.at[c])

    def halo(up):
        src = pl.ds(ROWS - 8 if up else 0, 8)
        dst = pl.ds(0 if up else ROWS + 8, 8)
        return pltpu.make_async_remote_copy(
            src_ref=field.at[:, :, :, src, :], dst_ref=padded.at[:, :, :, dst, :], send_sem=h_send.at[int(up)],
            recv_sem=h_recv.at[int(up)], device_id=(w + 1 if up else w - 1, me), device_id_type=MESH)

    send_lines(0)
    pl.when(w < WALLS - 1)(lambda: halo(True).start())
    pl.when(w > 0)(lambda: halo(False).start())
    send_lines(1)

    @pl.when(at_low)
    def _():
        padded[:, :, :, 0:8, :] = jnp.zeros((MODES, COMPS, 2, 8, COLS), jnp.float32)

    @pl.when(at_high)
    def _():
        padded[:, :, :, ROWS + 8 :, :] = jnp.zeros((MODES, COMPS, 2, 8, COLS), jnp.float32)

    for load in loads:
        load.wait()
    turned[...] = jnp.zeros((INNER, INNER), jnp.float32)
    turned[0:STEN, 0:ROWS] = sten[...]
    turned[STEN : STEN + 2, 0:ROWS] = flow[...]
    columns = turned[...].T
    for k in range(STEN + 2):
        coef[k] = jnp.broadcast_to(columns[0:ROWS, k : k + 1], (ROWS, INNER))

    pl.when(w > 0)(lambda: halo(True).wait_recv())
    pl.when(w < WALLS - 1)(lambda: halo(False).wait_recv())
    local_terms(0, padded, base, coef, kx)

    send_lines(2)

    take_lines(0)
    filter_lines(0, recv, ret, work, mid, pair, trig)
    send_back(0)
    local_terms(1, padded, base, coef, kx)
    take_lines(1)
    filter_lines(1, recv, ret, work, mid, pair, trig)
    send_back(1)
    local_terms(2, padded, base, coef, kx)
    base_copy = pltpu.make_async_copy(base, base_out, out_sem.at[0])
    base_copy.start()
    take_lines(2)
    filter_lines(2, recv, ret, work, mid, pair, trig)

    def share(t, slot):
        return pltpu.make_async_remote_copy(
            src_ref=grads.at[2], dst_ref=shares.at[slot], send_sem=s_send, recv_sem=s_recv,
            device_id=(w, t), device_id_type=MESH)

    take_back(0)

    @pl.when(at_edge)
    def _():
        rows = pl.ds(pl.multiple_of(jnp.where(at_low, 0, ROWS - 8), 8), 8)
        copy = pltpu.make_async_copy(spw.at[:, 0, :, rows, :], edge, edge_sem)
        copy.start()
        copy.wait()
        line = lax.broadcasted_iota(jnp.int32, (8, COLS), 0)
        weight = jnp.zeros((8, COLS), jnp.float32)
        for j in range(8):
            weight = jnp.where(line == j, jnp.where(at_low, wc[0, j], wc[1, 7 - j]), weight)
        patches = (lax.broadcasted_iota(jnp.int32, (INNER, COLS), 0) == patch[...]).astype(jnp.bfloat16)
        sums = []
        for m in range(MODES):
            for p in range(2):
                values = weight * (base[m, 0, p, rows, :] + edge[m, p])
                sums.append(jnp.sum(values, axis=0, keepdims=True))
        rest = jnp.concatenate(sums, axis=0)
        total = jnp.zeros((8, INNER), jnp.float32)
        for _ in range(3):
            part = rest.astype(jnp.bfloat16)
            rest = rest - part.astype(jnp.float32)
            total += lax.dot_general(part, patches, (((1,), (1,)), ((), ())), preferred_element_type=jnp.float32)
        grads[2] = total
        for offset in OFFSETS:
            share(span_of(offset), me).start()

    send_back(2)

    def spread(side, t):
        return pltpu.make_async_remote_copy(
            src_ref=grads.at[side], dst_ref=grads.at[side], send_sem=g_send, recv_sem=g_recv.at[side],
            device_id=(t, me), device_id_type=MESH)

    @pl.when(at_edge)
    def _():
        wait_bytes(shares.at[pl.ds(0, SPANS - 1)], s_recv)
        shares[me] = grads[2]
        total = shares[0]
        for s in range(1, SPANS):
            total += shares[s]
        grads[jnp.where(at_low, 0, 1)] = total

    @pl.when(at_low)
    def _():
        for t in range(1, WALLS):
            spread(0, t).start()

    @pl.when(at_high)
    def _():
        for t in range(WALLS - 1):
            spread(1, t).start()

    take_back(1)
    pl.when(jnp.logical_not(at_low))(lambda: spread(0, w).wait_recv())
    pl.when(jnp.logical_not(at_high))(lambda: spread(1, w).wait_recv())
    grad_copy = pltpu.make_async_copy(grads.at[pl.ds(0, 2)], grad_out, out_sem.at[1])
    grad_copy.start()

    wait_bytes(recv.at[:, pl.ds(0, SPANS - 1)], f_send)
    pl.when(w < WALLS - 1)(lambda: halo(True).wait_send())
    pl.when(w > 0)(lambda: halo(False).wait_send())

    @pl.when(at_edge)
    def _():
        wait_bytes(shares.at[pl.ds(0, SPANS - 1)], s_send)

        wait_bytes(shares.at[pl.ds(0, WALLS - 1)], g_send)

    base_copy.wait()
    grad_copy.wait()
    wait_bytes(ret.at[:, pl.ds(0, SPANS - 1)], r_send)
    take_back(2)


def on_device(field, mean_flow, d2_coef, wall_coef, kx_index, patch_of):
    pair, trig = tables()
    arrays = (field, mean_flow, d2_coef, wall_coef, kx_index, patch_of, pair, trig)
    whole = (MODES, COMPS, 2, ROWS, COLS)
    dma = pltpu.SemaphoreType.DMA
    base, spanwise, grads = pl.pallas_call(
        kernel,
        out_shape=[
            jax.ShapeDtypeStruct(whole, jnp.float32),
            jax.ShapeDtypeStruct(whole, jnp.float32),
            jax.ShapeDtypeStruct((2, 8, INNER), jnp.float32),
        ],
        in_specs=[pl.BlockSpec(memory_space=pl.ANY)] * 8,
        out_specs=[pl.BlockSpec(memory_space=pl.ANY)] * 3,
        scratch_shapes=[
            pltpu.VMEM((MODES, COMPS, 2, ROWS + 16, COLS), jnp.float32),
            pltpu.VMEM(whole, jnp.float32),
            pltpu.VMEM((COMPS, SPANS, 2, 8, COLS), jnp.float32),
            pltpu.VMEM((COMPS, SPANS, 2, 8, COLS), jnp.float32),
            pltpu.VMEM((OUTER, 8, 2 * INNER), jnp.float32),
            pltpu.VMEM((OUTER, 8, 2 * INNER), jnp.float32),
            pltpu.VMEM((2, 2, 2 * INNER, 2 * INNER), jnp.bfloat16),
            pltpu.VMEM((OUTER, 3, INNER), jnp.float32),
            pltpu.VMEM((STEN + 2, ROWS, INNER), jnp.float32),
            pltpu.VMEM((INNER, INNER), jnp.float32),
            pltpu.VMEM((2, ROWS), jnp.float32),
            pltpu.VMEM((STEN, ROWS), jnp.float32),
            pltpu.SMEM((2, 8), jnp.float32),
            pltpu.SMEM((MODES,), jnp.int32),
            pltpu.VMEM((1, COLS), jnp.int32),
            pltpu.VMEM((MODES, 2, 8, COLS), jnp.float32),
            pltpu.VMEM((3, 8, INNER), jnp.float32),
            pltpu.VMEM((SPANS, 8, INNER), jnp.float32),
            dma((8,)),
            dma,
            dma((COMPS,)),
            dma,
            dma((COMPS,)),
            dma((2,)),
            dma((2,)),
            dma,
            dma,
            dma,
            dma((2,)),
            dma((2,)),
            dma,
        ],
        compiler_params=pltpu.CompilerParams(collective_id=0, has_side_effects=True, vmem_limit_bytes=16 * 2**20),
    )(*[pltpu.with_memory_space_constraint(jnp.asarray(array), pltpu.HBM) for array in arrays])
    new_field = base + spanwise
    wall_grad = grads[:, :, :PATCH].reshape(2, MODES, 2, PATCH)
    return new_field, wall_grad


def solution(mesh):
    return jax.shard_map(
        on_device,
        mesh=mesh,
        in_specs=(
            P(None, None, None, "wall", "span"),
            P(None, "wall"),
            P(None, "wall"),
            P(),
            P(),
            P("span"),
        ),
        out_specs=(P(None, None, None, "wall", "span"), P()),
        check_vma=False,
    )
```

```python
import math

import jax
import jax.numpy as jnp
import numpy as np
from jax import lax
from jax.experimental import pallas as pl
from jax.experimental.pallas import tpu as pltpu
from jax.sharding import PartitionSpec as P

MESH = pl.DeviceIdType.MESH
MODES, COMPS, ROWS, COLS = 4, 3, 32, 384
WALLS, SPANS = 16, 16
STEN = 15
PATCH = 64
NZ = SPANS * COLS
INNER = 128
OUTER = NZ // INNER
CUTOFF = NZ // 3
VIS = 0.5
TAU = 0.25

OFFSETS = sorted(
    [(hi, z) for hi in range(2) for z in range(8) if hi or z],
    key=lambda o: (-min(o[1], 8 - o[1]), -o[0], o),
)


def tables():
    outer = np.array([next(k for k in range(OUTER) if k % 16 == i // 3 and k % 3 == i % 3) for i in range(OUTER)])
    inner = np.arange(INNER)
    angle = 2.0 * np.pi * (outer[:, None] * inner[None, :] % NZ) / NZ
    twist = np.stack([np.cos(angle), np.sin(angle)], axis=1)
    wave = outer[:, None] + OUTER * inner[None, :]
    signed = np.where(wave > NZ // 2, wave - NZ, wave)
    factor = np.where(np.abs(signed) < CUTOFF, -VIS * (signed / CUTOFF) ** 2, 0.0) / NZ
    angle = 2.0 * np.pi * (inner[:, None] * inner[None, :] % INNER) / INNER
    c, s = np.cos(angle), np.sin(angle)
    pair = []
    for table in (np.block([[c, -s], [s, c]]), np.block([[c, s], [-s, c]])):
        high = table.astype(np.float32).astype(jnp.bfloat16)
        low = (table - high.astype(np.float64)).astype(np.float32).astype(jnp.bfloat16)
        pair.append(np.stack([high, low]))
    rows = np.concatenate([twist, factor[:, None]], axis=1).astype(np.float32)
    return np.stack(pair), rows


def times(value, cos, sin):
    re, im = value
    half = math.sqrt(0.5)
    if abs(sin) < 1e-12:
        return (re, im) if cos > 0 else (-re, -im)
    if abs(cos) < 1e-12:
        return (im, -re) if sin > 0 else (-im, re)
    if abs(abs(cos) - half) < 1e-12 and abs(abs(sin) - half) < 1e-12:
        a, b = math.copysign(half, cos), math.copysign(half, sin)
        if a == b:
            return ((re + im) * a, (im - re) * a)
        return ((re - im) * a, (im + re) * a)
    return (re * cos + im * sin, im * cos - re * sin)


def transform(values):
    n = len(values)
    if n == 1:
        return values
    even, odd = transform(values[0::2]), transform(values[1::2])
    first, second = [], []
    for k in range(n // 2):
        a = 2.0 * math.pi * k / n
        t = times(odd[k], math.cos(a), math.sin(a))
        first.append((even[k][0] + t[0], even[k][1] + t[1]))
        second.append((even[k][0] - t[0], even[k][1] - t[1]))
    return first + second


def transform_three(x):
    (ar, ai), (br, bi), (cr, ci) = x
    sr, si, dr, di = br + cr, bi + ci, br - cr, bi - ci
    mr, mi = ar - 0.5 * sr, ai - 0.5 * si
    h = math.sqrt(0.75)
    return [(ar + sr, ai + si), (mr + h * di, mi - h * dr), (mr - h * di, mi + h * dr)]


def swap(values):
    return [(im, re) for re, im in values]


def multiply(values, pair_ref, which):
    high = values.astype(jnp.bfloat16)
    low = (values - high.astype(jnp.float32)).astype(jnp.bfloat16)
    out = jnp.dot(high, pair_ref[which, 0], preferred_element_type=jnp.float32)
    out += jnp.dot(low, pair_ref[which, 0], preferred_element_type=jnp.float32)
    out += jnp.dot(high, pair_ref[which, 1], preferred_element_type=jnp.float32)
    return out


def filter_lines(c, recv, ret, work, mid, pair, trig):
    def lanes(j):
        return slice(INNER * j, INNER * (j + 1))

    for j in range(3):
        order = [(i + 5 * j) % 16 for i in range(16)]
        out = transform([(recv[c, s, 0, :, lanes(j)], recv[c, s, 1, :, lanes(j)]) for s in order])
        for k in range(16):
            work[3 * k + j, :, :INNER], work[3 * k + j, :, INNER:] = out[k]
    for k in range(16):
        out = transform_three([(work[3 * k + j, :, :INNER], work[3 * k + j, :, INNER:]) for j in range(3)])
        for i, (re, im) in enumerate(out):
            cos, sin = trig[3 * k + i, 0:1, :], trig[3 * k + i, 1:2, :]
            mid[3 * k + i, :, :INNER] = re * cos + im * sin
            mid[3 * k + i, :, INNER:] = im * cos - re * sin
    modes = multiply(mid[...].reshape(OUTER * 8, 2 * INNER), pair, 0).reshape(OUTER, 8, 2 * INNER)
    work[...] = modes
    for k in range(OUTER):
        factor = trig[k, 2:3, :]
        mid[k, :, :INNER] = work[k, :, :INNER] * factor
        mid[k, :, INNER:] = work[k, :, INNER:] * factor
    work[...] = multiply(mid[...].reshape(OUTER * 8, 2 * INNER), pair, 1).reshape(OUTER, 8, 2 * INNER)
    for k in range(16):
        values = []
        for i in range(3):
            re, im = work[3 * k + i, :, :INNER], work[3 * k + i, :, INNER:]
            cos, sin = trig[3 * k + i, 0:1, :], trig[3 * k + i, 1:2, :]
            values.append((re * cos - im * sin, im * cos + re * sin))
        out = swap(transform_three(swap(values)))
        for j in range(3):
            mid[3 * k + j, :, :INNER], mid[3 * k + j, :, INNER:] = out[j]
    for j in range(3):
        order = [(i + 5 * j) % 16 for i in range(16)]
        out = swap(transform(swap([(mid[3 * k + j, :, :INNER], mid[3 * k + j, :, INNER:]) for k in range(16)])))
        for i, s in enumerate(order):
            ret[c, s, 0, :, lanes(j)], ret[c, s, 1, :, lanes(j)] = out[i]


def local_terms(c, padded, base, coef, wave_ref):
    def body(i, carry):
        m, j = i // 3, i % 3
        lanes = pl.ds(pl.multiple_of(j * INNER, INNER), INNER)
        rate = TAU * 0.25 * wave_ref[m].astype(jnp.float32)
        for octet in range(ROWS // 8):
            rows = slice(8 * octet, 8 * octet + 8)
            sums = []
            for p in range(2):
                total = jnp.zeros((8, INNER), jnp.float32)
                for s in range(STEN):
                    total += coef[s, rows, :] * padded[m, c, p, 8 * octet + 1 + s : 8 * octet + 9 + s, lanes]
                sums.append(total)
            here = slice(8 * octet + 8, 8 * octet + 16)
            re, im = padded[m, c, 0, here, lanes], padded[m, c, 1, here, lanes]
            turn = rate * coef[STEN, rows, :]
            sums[0] += re - turn * im
            sums[1] += im + turn * re
            if c == 1:
                couple = TAU * coef[STEN + 1, rows, :]
                for p in range(2):
                    sums[p] -= couple * padded[m, 0, p, here, lanes]
            for p in range(2):
                base[m, c, p, rows, lanes] = sums[p]
        return carry

    lax.fori_loop(0, MODES * 3, body, 0)


def kernel(
    field, mean_flow, d2_coef, wall_coef, kx_index, patch_of, pair_hbm, trig_hbm,
    base_out, spw, grad_out,
    padded, base, recv, ret, work, mid, pair, trig, coef, turned, flow, sten, wc, kx, patch, edge, grads, shares,
    load_sem, f_send, f_recv, r_send, r_recv, h_send, h_recv, s_send, s_recv, g_send, g_recv,
    out_sem, edge_sem,
):
    w, me = lax.axis_index("wall"), lax.axis_index("span")
    at_low, at_high = w == 0, w == WALLS - 1
    at_edge = jnp.logical_or(at_low, at_high)

    def span_of(offset, sign=1):
        hi = lax.rem(me // 8 + offset[0], 2)
        return hi * 8 + lax.rem(lax.rem(me, 8) + 8 + sign * offset[1], 8)

    loads = [
        pltpu.make_async_copy(field, padded.at[:, :, :, pl.ds(8, ROWS), :], load_sem.at[0]),
        pltpu.make_async_copy(mean_flow, flow, load_sem.at[1]),
        pltpu.make_async_copy(d2_coef, sten, load_sem.at[2]),
        pltpu.make_async_copy(wall_coef, wc, load_sem.at[3]),
        pltpu.make_async_copy(kx_index, kx, load_sem.at[4]),
        pltpu.make_async_copy(patch_of, patch.at[0], load_sem.at[5]),
        pltpu.make_async_copy(pair_hbm, pair, load_sem.at[6]),
        pltpu.make_async_copy(trig_hbm, trig, load_sem.at[7]),
    ]

    barrier = pltpu.get_barrier_semaphore()
    for offset in OFFSETS:
        pl.semaphore_signal(barrier, inc=1, device_id=(w, span_of(offset)), device_id_type=MESH)

    def greet(wall):
        pl.semaphore_signal(barrier, inc=1, device_id=(wall, me), device_id_type=MESH)

    pl.when(w > 0)(lambda: greet(w - 1))
    pl.when(w < WALLS - 1)(lambda: greet(w + 1))
    pl.when(w > 1)(lambda: greet(0))
    pl.when(w < WALLS - 2)(lambda: greet(WALLS - 1))
    for load in loads:
        load.start()
    pl.when(at_edge)(lambda: pl.semaphore_wait(barrier, SPANS - 1 + WALLS - 1))
    pl.when(jnp.logical_not(at_edge))(lambda: pl.semaphore_wait(barrier, SPANS - 1 + 2))

    def block(t, c):
        return (t // 4, c, slice(None), pl.ds(pl.multiple_of(8 * lax.rem(t, 4), 8), 8), slice(None))

    def forward(c, t, slot):
        return pltpu.make_async_remote_copy(
            src_ref=field.at[block(t, c)], dst_ref=recv.at[c, slot], send_sem=f_send,
            recv_sem=f_recv.at[c], device_id=(w, t), device_id_type=MESH)

    def backward(c, t, slot):
        return pltpu.make_async_remote_copy(
            src_ref=ret.at[c, t], dst_ref=spw.at[block(slot, c)], send_sem=r_send,
            recv_sem=r_recv.at[c], device_id=(w, t), device_id_type=MESH)

    def wait_bytes(ref, sem):
        pltpu.make_async_copy(ref, ref, sem).wait()

    def own(c):
        return pltpu.make_async_copy(field.at[block(me, c)], recv.at[c, me], f_recv.at[c])

    def own_back(c):
        return pltpu.make_async_copy(ret.at[c, me], spw.at[block(me, c)], r_recv.at[c])

    def send_lines(c):
        for offset in OFFSETS:
            forward(c, span_of(offset), me).start()
        own(c).start()

    def take_lines(c):
        wait_bytes(recv.at[c], f_recv.at[c])

    def send_back(c):
        for offset in OFFSETS:
            backward(c, span_of(offset), me).start()
        own_back(c).start()

    def take_back(c):
        wait_bytes(spw.at[:, c], r_recv.at[c])

    def halo(up):
        src = pl.ds(ROWS - 8 if up else 0, 8)
        dst = pl.ds(0 if up else ROWS + 8, 8)
        return pltpu.make_async_remote_copy(
            src_ref=field.at[:, :, :, src, :], dst_ref=padded.at[:, :, :, dst, :], send_sem=h_send.at[int(up)],
            recv_sem=h_recv.at[int(up)], device_id=(w + 1 if up else w - 1, me), device_id_type=MESH)

    send_lines(0)
    pl.when(w < WALLS - 1)(lambda: halo(True).start())
    pl.when(w > 0)(lambda: halo(False).start())
    send_lines(1)

    @pl.when(at_low)
    def _():
        padded[:, :, :, 0:8, :] = jnp.zeros((MODES, COMPS, 2, 8, COLS), jnp.float32)

    @pl.when(at_high)
    def _():
        padded[:, :, :, ROWS + 8 :, :] = jnp.zeros((MODES, COMPS, 2, 8, COLS), jnp.float32)

    for load in loads:
        load.wait()
    turned[...] = jnp.zeros((INNER, INNER), jnp.float32)
    turned[0:STEN, 0:ROWS] = sten[...]
    turned[STEN : STEN + 2, 0:ROWS] = flow[...]
    columns = turned[...].T
    for k in range(STEN + 2):
        coef[k] = jnp.broadcast_to(columns[0:ROWS, k : k + 1], (ROWS, INNER))

    pl.when(w > 0)(lambda: halo(True).wait_recv())
    pl.when(w < WALLS - 1)(lambda: halo(False).wait_recv())
    local_terms(0, padded, base, coef, kx)

    send_lines(2)

    take_lines(0)
    filter_lines(0, recv, ret, work, mid, pair, trig)
    send_back(0)
    local_terms(1, padded, base, coef, kx)
    take_lines(1)
    filter_lines(1, recv, ret, work, mid, pair, trig)
    send_back(1)
    local_terms(2, padded, base, coef, kx)
    base_copy = pltpu.make_async_copy(base, base_out, out_sem.at[0])
    base_copy.start()
    take_lines(2)
    filter_lines(2, recv, ret, work, mid, pair, trig)

    def share(t, slot):
        return pltpu.make_async_remote_copy(
            src_ref=grads.at[2], dst_ref=shares.at[slot], send_sem=s_send, recv_sem=s_recv,
            device_id=(w, t), device_id_type=MESH)

    take_back(0)

    @pl.when(at_edge)
    def _():
        rows = pl.ds(pl.multiple_of(jnp.where(at_low, 0, ROWS - 8), 8), 8)
        copy = pltpu.make_async_copy(spw.at[:, 0, :, rows, :], edge, edge_sem)
        copy.start()
        copy.wait()
        line = lax.broadcasted_iota(jnp.int32, (8, COLS), 0)
        weight = jnp.zeros((8, COLS), jnp.float32)
        for j in range(8):
            weight = jnp.where(line == j, jnp.where(at_low, wc[0, j], wc[1, 7 - j]), weight)
        patches = (lax.broadcasted_iota(jnp.int32, (INNER, COLS), 0) == patch[...]).astype(jnp.bfloat16)
        sums = []
        for m in range(MODES):
            for p in range(2):
                values = weight * (base[m, 0, p, rows, :] + edge[m, p])
                sums.append(jnp.sum(values, axis=0, keepdims=True))
        rest = jnp.concatenate(sums, axis=0)
        total = jnp.zeros((8, INNER), jnp.float32)
        for _ in range(3):
            part = rest.astype(jnp.bfloat16)
            rest = rest - part.astype(jnp.float32)
            total += lax.dot_general(part, patches, (((1,), (1,)), ((), ())), preferred_element_type=jnp.float32)
        grads[2] = total
        for offset in OFFSETS:
            share(span_of(offset), me).start()

    send_back(2)

    def spread(side, t):
        return pltpu.make_async_remote_copy(
            src_ref=grads.at[side], dst_ref=grads.at[side], send_sem=g_send, recv_sem=g_recv.at[side],
            device_id=(t, me), device_id_type=MESH)

    @pl.when(at_edge)
    def _():
        wait_bytes(shares.at[pl.ds(0, SPANS - 1)], s_recv)
        shares[me] = grads[2]
        total = shares[0]
        for s in range(1, SPANS):
            total += shares[s]
        grads[jnp.where(at_low, 0, 1)] = total

    @pl.when(at_low)
    def _():
        for t in range(1, WALLS):
            spread(0, t).start()

    @pl.when(at_high)
    def _():
        for t in range(WALLS - 1):
            spread(1, t).start()

    take_back(1)
    pl.when(jnp.logical_not(at_low))(lambda: spread(0, w).wait_recv())
    pl.when(jnp.logical_not(at_high))(lambda: spread(1, w).wait_recv())
    grad_copy = pltpu.make_async_copy(grads.at[pl.ds(0, 2)], grad_out, out_sem.at[1])
    grad_copy.start()

    wait_bytes(recv.at[:, pl.ds(0, SPANS - 1)], f_send)
    pl.when(w < WALLS - 1)(lambda: halo(True).wait_send())
    pl.when(w > 0)(lambda: halo(False).wait_send())

    @pl.when(at_edge)
    def _():
        wait_bytes(shares.at[pl.ds(0, SPANS - 1)], s_send)

        wait_bytes(shares.at[pl.ds(0, WALLS - 1)], g_send)

    base_copy.wait()
    grad_copy.wait()
    wait_bytes(ret.at[:, pl.ds(0, SPANS - 1)], r_send)
    take_back(2)


def on_device(field, mean_flow, d2_coef, wall_coef, kx_index, patch_of):
    pair, trig = tables()
    arrays = (field, mean_flow, d2_coef, wall_coef, kx_index, patch_of, pair, trig)
    whole = (MODES, COMPS, 2, ROWS, COLS)
    dma = pltpu.SemaphoreType.DMA
    base, spanwise, grads = pl.pallas_call(
        kernel,
        out_shape=[
            jax.ShapeDtypeStruct(whole, jnp.float32),
            jax.ShapeDtypeStruct(whole, jnp.float32),
            jax.ShapeDtypeStruct((2, 8, INNER), jnp.float32),
        ],
        in_specs=[pl.BlockSpec(memory_space=pl.ANY)] * 8,
        out_specs=[pl.BlockSpec(memory_space=pl.ANY)] * 3,
        scratch_shapes=[
            pltpu.VMEM((MODES, COMPS, 2, ROWS + 16, COLS), jnp.float32),
            pltpu.VMEM(whole, jnp.float32),
            pltpu.VMEM((COMPS, SPANS, 2, 8, COLS), jnp.float32),
            pltpu.VMEM((COMPS, SPANS, 2, 8, COLS), jnp.float32),
            pltpu.VMEM((OUTER, 8, 2 * INNER), jnp.float32),
            pltpu.VMEM((OUTER, 8, 2 * INNER), jnp.float32),
            pltpu.VMEM((2, 2, 2 * INNER, 2 * INNER), jnp.bfloat16),
            pltpu.VMEM((OUTER, 3, INNER), jnp.float32),
            pltpu.VMEM((STEN + 2, ROWS, INNER), jnp.float32),
            pltpu.VMEM((INNER, INNER), jnp.float32),
            pltpu.VMEM((2, ROWS), jnp.float32),
            pltpu.VMEM((STEN, ROWS), jnp.float32),
            pltpu.SMEM((2, 8), jnp.float32),
            pltpu.SMEM((MODES,), jnp.int32),
            pltpu.VMEM((1, COLS), jnp.int32),
            pltpu.VMEM((MODES, 2, 8, COLS), jnp.float32),
            pltpu.VMEM((3, 8, INNER), jnp.float32),
            pltpu.VMEM((SPANS, 8, INNER), jnp.float32),
            dma((8,)),
            dma,
            dma((COMPS,)),
            dma,
            dma((COMPS,)),
            dma((2,)),
            dma((2,)),
            dma,
            dma,
            dma,
            dma((2,)),
            dma((2,)),
            dma,
        ],
        compiler_params=pltpu.CompilerParams(collective_id=0, has_side_effects=True, vmem_limit_bytes=16 * 2**20),
    )(*[pltpu.with_memory_space_constraint(jnp.asarray(array), pltpu.HBM) for array in arrays])
    new_field = base + spanwise
    wall_grad = grads[:, :, :PATCH].reshape(2, MODES, 2, PATCH)
    return new_field, wall_grad


def solution(mesh):
    return jax.shard_map(
        on_device,
        mesh=mesh,
        in_specs=(
            P(None, None, None, "wall", "span"),
            P(None, "wall"),
            P(None, "wall"),
            P(),
            P(),
            P("span"),
        ),
        out_specs=(P(None, None, None, "wall", "span"), P()),
        check_vma=False,
    )
```

```python
import math

import jax
import jax.numpy as jnp
import numpy as np
from jax import lax
from jax.experimental import pallas as pl
from jax.experimental.pallas import tpu as pltpu
from jax.sharding import PartitionSpec as P

MESH = pl.DeviceIdType.MESH
MODES, COMPS, ROWS, COLS = 4, 3, 32, 384
WALLS, SPANS = 16, 16
STEN = 15
PATCH = 64
NZ = SPANS * COLS
INNER = 128
OUTER = NZ // INNER
CUTOFF = NZ // 3
VIS = 0.5
TAU = 0.25

OFFSETS = sorted(
    [(hi, z) for hi in range(2) for z in range(8) if hi or z],
    key=lambda o: (2 * o[0] + min(o[1], 8 - o[1]), o),
)


def tables():
    outer = np.array([next(k for k in range(OUTER) if k % 16 == i // 3 and k % 3 == i % 3) for i in range(OUTER)])
    inner = np.arange(INNER)
    angle = 2.0 * np.pi * (outer[:, None] * inner[None, :] % NZ) / NZ
    twist = np.stack([np.cos(angle), np.sin(angle)], axis=1)
    wave = outer[:, None] + OUTER * inner[None, :]
    signed = np.where(wave > NZ // 2, wave - NZ, wave)
    factor = np.where(np.abs(signed) < CUTOFF, -VIS * (signed / CUTOFF) ** 2, 0.0) / NZ
    angle = 2.0 * np.pi * (inner[:, None] * inner[None, :] % INNER) / INNER
    c, s = np.cos(angle), np.sin(angle)
    pair = []
    for table in (np.block([[c, -s], [s, c]]), np.block([[c, s], [-s, c]])):
        high = table.astype(np.float32).astype(jnp.bfloat16)
        low = (table - high.astype(np.float64)).astype(np.float32).astype(jnp.bfloat16)
        pair.append(np.stack([high, low]))
    rows = np.concatenate([twist, factor[:, None]], axis=1).astype(np.float32)
    return np.stack(pair), rows


def times(value, cos, sin):
    re, im = value
    half = math.sqrt(0.5)
    if abs(sin) < 1e-12:
        return (re, im) if cos > 0 else (-re, -im)
    if abs(cos) < 1e-12:
        return (im, -re) if sin > 0 else (-im, re)
    if abs(abs(cos) - half) < 1e-12 and abs(abs(sin) - half) < 1e-12:
        a, b = math.copysign(half, cos), math.copysign(half, sin)
        if a == b:
            return ((re + im) * a, (im - re) * a)
        return ((re - im) * a, (im + re) * a)
    return (re * cos + im * sin, im * cos - re * sin)


def transform(values):
    n = len(values)
    if n == 1:
        return values
    even, odd = transform(values[0::2]), transform(values[1::2])
    first, second = [], []
    for k in range(n // 2):
        a = 2.0 * math.pi * k / n
        t = times(odd[k], math.cos(a), math.sin(a))
        first.append((even[k][0] + t[0], even[k][1] + t[1]))
        second.append((even[k][0] - t[0], even[k][1] - t[1]))
    return first + second


def transform_three(x):
    (ar, ai), (br, bi), (cr, ci) = x
    sr, si, dr, di = br + cr, bi + ci, br - cr, bi - ci
    mr, mi = ar - 0.5 * sr, ai - 0.5 * si
    h = math.sqrt(0.75)
    return [(ar + sr, ai + si), (mr + h * di, mi - h * dr), (mr - h * di, mi + h * dr)]


def swap(values):
    return [(im, re) for re, im in values]


def multiply(values, pair_ref, which):
    high = values.astype(jnp.bfloat16)
    low = (values - high.astype(jnp.float32)).astype(jnp.bfloat16)
    out = jnp.dot(high, pair_ref[which, 0], preferred_element_type=jnp.float32)
    out += jnp.dot(low, pair_ref[which, 0], preferred_element_type=jnp.float32)
    out += jnp.dot(high, pair_ref[which, 1], preferred_element_type=jnp.float32)
    return out


def filter_lines(c, recv, ret, work, mid, pair, trig):
    def lanes(j):
        return slice(INNER * j, INNER * (j + 1))

    for j in range(3):
        order = [(i + 5 * j) % 16 for i in range(16)]
        out = transform([(recv[c, s, 0, :, lanes(j)], recv[c, s, 1, :, lanes(j)]) for s in order])
        for k in range(16):
            work[3 * k + j, :, :INNER], work[3 * k + j, :, INNER:] = out[k]
    for k in range(16):
        out = transform_three([(work[3 * k + j, :, :INNER], work[3 * k + j, :, INNER:]) for j in range(3)])
        for i, (re, im) in enumerate(out):
            cos, sin = trig[3 * k + i, 0:1, :], trig[3 * k + i, 1:2, :]
            mid[3 * k + i, :, :INNER] = re * cos + im * sin
            mid[3 * k + i, :, INNER:] = im * cos - re * sin
    modes = multiply(mid[...].reshape(OUTER * 8, 2 * INNER), pair, 0).reshape(OUTER, 8, 2 * INNER)
    work[...] = modes
    for k in range(OUTER):
        factor = trig[k, 2:3, :]
        mid[k, :, :INNER] = work[k, :, :INNER] * factor
        mid[k, :, INNER:] = work[k, :, INNER:] * factor
    work[...] = multiply(mid[...].reshape(OUTER * 8, 2 * INNER), pair, 1).reshape(OUTER, 8, 2 * INNER)
    for k in range(16):
        values = []
        for i in range(3):
            re, im = work[3 * k + i, :, :INNER], work[3 * k + i, :, INNER:]
            cos, sin = trig[3 * k + i, 0:1, :], trig[3 * k + i, 1:2, :]
            values.append((re * cos - im * sin, im * cos + re * sin))
        out = swap(transform_three(swap(values)))
        for j in range(3):
            mid[3 * k + j, :, :INNER], mid[3 * k + j, :, INNER:] = out[j]
    for j in range(3):
        order = [(i + 5 * j) % 16 for i in range(16)]
        out = swap(transform(swap([(mid[3 * k + j, :, :INNER], mid[3 * k + j, :, INNER:]) for k in range(16)])))
        for i, s in enumerate(order):
            ret[c, s, 0, :, lanes(j)], ret[c, s, 1, :, lanes(j)] = out[i]


def local_terms(c, padded, base, coef, wave_ref):
    def body(i, carry):
        m, j = i // 3, i % 3
        lanes = pl.ds(pl.multiple_of(j * INNER, INNER), INNER)
        rate = TAU * 0.25 * wave_ref[m].astype(jnp.float32)
        for octet in range(ROWS // 8):
            rows = slice(8 * octet, 8 * octet + 8)
            sums = []
            for p in range(2):
                total = jnp.zeros((8, INNER), jnp.float32)
                for s in range(STEN):
                    total += coef[s, rows, :] * padded[m, c, p, 8 * octet + 1 + s : 8 * octet + 9 + s, lanes]
                sums.append(total)
            here = slice(8 * octet + 8, 8 * octet + 16)
            re, im = padded[m, c, 0, here, lanes], padded[m, c, 1, here, lanes]
            turn = rate * coef[STEN, rows, :]
            sums[0] += re - turn * im
            sums[1] += im + turn * re
            if c == 1:
                couple = TAU * coef[STEN + 1, rows, :]
                for p in range(2):
                    sums[p] -= couple * padded[m, 0, p, here, lanes]
            for p in range(2):
                base[m, c, p, rows, lanes] = sums[p]
        return carry

    lax.fori_loop(0, MODES * 3, body, 0)


def kernel(
    field, mean_flow, d2_coef, wall_coef, kx_index, patch_of, pair_hbm, trig_hbm,
    base_out, spw, grad_out,
    padded, base, recv, ret, work, mid, pair, trig, coef, turned, flow, sten, wc, kx, patch, edge, grads, shares,
    load_sem, f_send, f_recv, r_send, r_recv, h_send, h_recv, s_send, s_recv, g_send, g_recv,
    out_sem, edge_sem, ready,
):
    w, me = lax.axis_index("wall"), lax.axis_index("span")
    at_low, at_high = w == 0, w == WALLS - 1
    at_edge = jnp.logical_or(at_low, at_high)

    def span_of(offset, sign=1):
        hi = lax.rem(me // 8 + offset[0], 2)
        return hi * 8 + lax.rem(lax.rem(me, 8) + 8 + sign * offset[1], 8)

    loads = [
        pltpu.make_async_copy(field, padded.at[:, :, :, pl.ds(8, ROWS), :], load_sem.at[0]),
        pltpu.make_async_copy(mean_flow, flow, load_sem.at[1]),
        pltpu.make_async_copy(d2_coef, sten, load_sem.at[2]),
        pltpu.make_async_copy(wall_coef, wc, load_sem.at[3]),
        pltpu.make_async_copy(kx_index, kx, load_sem.at[4]),
        pltpu.make_async_copy(patch_of, patch.at[0], load_sem.at[5]),
        pltpu.make_async_copy(pair_hbm, pair, load_sem.at[6]),
        pltpu.make_async_copy(trig_hbm, trig, load_sem.at[7]),
    ]

    barrier = pltpu.get_barrier_semaphore()
    for offset in OFFSETS:
        pl.semaphore_signal(barrier, inc=1, device_id=(w, span_of(offset)), device_id_type=MESH)

    def greet(wall):
        pl.semaphore_signal(barrier, inc=1, device_id=(wall, me), device_id_type=MESH)

    pl.when(w > 0)(lambda: greet(w - 1))
    pl.when(w < WALLS - 1)(lambda: greet(w + 1))

    @pl.when(at_low)
    def _():
        for t in range(2, WALLS):
            greet(t)

    @pl.when(at_high)
    def _():
        for t in range(WALLS - 2):
            greet(t)

    for load in loads:
        load.start()
    near = [w > 0, w > 1, w < WALLS - 1, w < WALLS - 2]
    pl.semaphore_wait(barrier, SPANS - 1 + sum(one.astype(jnp.int32) for one in near))

    def block(t, c):
        return (t // 4, c, slice(None), pl.ds(pl.multiple_of(8 * lax.rem(t, 4), 8), 8), slice(None))

    def forward(c, t, slot):
        return pltpu.make_async_remote_copy(
            src_ref=field.at[block(t, c)], dst_ref=recv.at[c, slot], send_sem=f_send,
            recv_sem=f_recv.at[c], device_id=(w, t), device_id_type=MESH)

    def backward(c, t, slot):
        return pltpu.make_async_remote_copy(
            src_ref=ret.at[c, t], dst_ref=spw.at[block(slot, c)], send_sem=r_send,
            recv_sem=r_recv.at[c], device_id=(w, t), device_id_type=MESH)

    def wait_bytes(ref, sem):
        pltpu.make_async_copy(ref, ref, sem).wait()

    def own(c):
        return pltpu.make_async_copy(field.at[block(me, c)], recv.at[c, me], f_recv.at[c])

    def own_back(c):
        return pltpu.make_async_copy(ret.at[c, me], spw.at[block(me, c)], r_recv.at[c])

    def send_lines(c):
        for offset in OFFSETS:
            forward(c, span_of(offset), me).start()
        own(c).start()

    def take_lines(c):
        wait_bytes(recv.at[c], f_recv.at[c])

    def send_back(c):
        for offset in OFFSETS:
            backward(c, span_of(offset), me).start()
        own_back(c).start()

    def take_back(c):
        wait_bytes(spw.at[:, c], r_recv.at[c])

    def halo(up):
        src = pl.ds(ROWS - 8 if up else 0, 8)
        dst = pl.ds(0 if up else ROWS + 8, 8)
        return pltpu.make_async_remote_copy(
            src_ref=field.at[:, :, :, src, :], dst_ref=padded.at[:, :, :, dst, :], send_sem=h_send.at[int(up)],
            recv_sem=h_recv.at[int(up)], device_id=(w + 1 if up else w - 1, me), device_id_type=MESH)

    send_lines(0)
    pl.when(w < WALLS - 1)(lambda: halo(True).start())
    pl.when(w > 0)(lambda: halo(False).start())
    send_lines(1)

    def report(wall):
        pl.semaphore_signal(ready, inc=1, device_id=(wall, me), device_id_type=MESH)

    pl.when(w > 1)(lambda: report(0))
    pl.when(w < WALLS - 2)(lambda: report(WALLS - 1))

    @pl.when(at_low)
    def _():
        padded[:, :, :, 0:8, :] = jnp.zeros((MODES, COMPS, 2, 8, COLS), jnp.float32)

    @pl.when(at_high)
    def _():
        padded[:, :, :, ROWS + 8 :, :] = jnp.zeros((MODES, COMPS, 2, 8, COLS), jnp.float32)

    for load in loads:
        load.wait()
    turned[...] = jnp.zeros((INNER, INNER), jnp.float32)
    turned[0:STEN, 0:ROWS] = sten[...]
    turned[STEN : STEN + 2, 0:ROWS] = flow[...]
    columns = turned[...].T
    for k in range(STEN + 2):
        coef[k] = jnp.broadcast_to(columns[0:ROWS, k : k + 1], (ROWS, INNER))

    pl.when(w > 0)(lambda: halo(True).wait_recv())
    pl.when(w < WALLS - 1)(lambda: halo(False).wait_recv())
    local_terms(0, padded, base, coef, kx)

    send_lines(2)

    take_lines(0)
    filter_lines(0, recv, ret, work, mid, pair, trig)
    send_back(0)
    local_terms(1, padded, base, coef, kx)
    take_lines(1)
    filter_lines(1, recv, ret, work, mid, pair, trig)
    send_back(1)
    local_terms(2, padded, base, coef, kx)
    base_copy = pltpu.make_async_copy(base, base_out, out_sem.at[0])
    base_copy.start()
    take_lines(2)
    filter_lines(2, recv, ret, work, mid, pair, trig)

    def share(t, slot):
        return pltpu.make_async_remote_copy(
            src_ref=grads.at[2], dst_ref=shares.at[slot], send_sem=s_send, recv_sem=s_recv,
            device_id=(w, t), device_id_type=MESH)

    take_back(0)

    @pl.when(at_edge)
    def _():
        rows = pl.ds(pl.multiple_of(jnp.where(at_low, 0, ROWS - 8), 8), 8)
        copy = pltpu.make_async_copy(spw.at[:, 0, :, rows, :], edge, edge_sem)
        copy.start()
        copy.wait()
        line = lax.broadcasted_iota(jnp.int32, (8, COLS), 0)
        weight = jnp.zeros((8, COLS), jnp.float32)
        for j in range(8):
            weight = jnp.where(line == j, jnp.where(at_low, wc[0, j], wc[1, 7 - j]), weight)
        patches = (lax.broadcasted_iota(jnp.int32, (INNER, COLS), 0) == patch[...]).astype(jnp.bfloat16)
        sums = []
        for m in range(MODES):
            for p in range(2):
                values = weight * (base[m, 0, p, rows, :] + edge[m, p])
                sums.append(jnp.sum(values, axis=0, keepdims=True))
        rest = jnp.concatenate(sums, axis=0)
        total = jnp.zeros((8, INNER), jnp.float32)
        for _ in range(3):
            part = rest.astype(jnp.bfloat16)
            rest = rest - part.astype(jnp.float32)
            total += lax.dot_general(part, patches, (((1,), (1,)), ((), ())), preferred_element_type=jnp.float32)
        grads[2] = total
        for offset in OFFSETS:
            share(span_of(offset), me).start()

    send_back(2)

    def spread(side, t):
        return pltpu.make_async_remote_copy(
            src_ref=grads.at[side], dst_ref=grads.at[side], send_sem=g_send, recv_sem=g_recv.at[side],
            device_id=(t, me), device_id_type=MESH)

    @pl.when(at_edge)
    def _():
        wait_bytes(shares.at[pl.ds(0, SPANS - 1)], s_recv)
        shares[me] = grads[2]
        total = shares[0]
        for s in range(1, SPANS):
            total += shares[s]
        grads[jnp.where(at_low, 0, 1)] = total
        pl.semaphore_wait(ready, WALLS - 2)

    @pl.when(at_low)
    def _():
        for t in range(1, WALLS):
            spread(0, t).start()

    @pl.when(at_high)
    def _():
        for t in range(WALLS - 1):
            spread(1, t).start()

    take_back(1)
    pl.when(jnp.logical_not(at_low))(lambda: spread(0, w).wait_recv())
    pl.when(jnp.logical_not(at_high))(lambda: spread(1, w).wait_recv())
    grad_copy = pltpu.make_async_copy(grads.at[pl.ds(0, 2)], grad_out, out_sem.at[1])
    grad_copy.start()

    wait_bytes(recv.at[:, pl.ds(0, SPANS - 1)], f_send)
    pl.when(w < WALLS - 1)(lambda: halo(True).wait_send())
    pl.when(w > 0)(lambda: halo(False).wait_send())

    @pl.when(at_edge)
    def _():
        wait_bytes(shares.at[pl.ds(0, SPANS - 1)], s_send)

        wait_bytes(shares.at[pl.ds(0, WALLS - 1)], g_send)

    base_copy.wait()
    grad_copy.wait()
    wait_bytes(ret.at[:, pl.ds(0, SPANS - 1)], r_send)
    take_back(2)


def on_device(field, mean_flow, d2_coef, wall_coef, kx_index, patch_of):
    pair, trig = tables()
    arrays = (field, mean_flow, d2_coef, wall_coef, kx_index, patch_of, pair, trig)
    whole = (MODES, COMPS, 2, ROWS, COLS)
    dma = pltpu.SemaphoreType.DMA
    base, spanwise, grads = pl.pallas_call(
        kernel,
        out_shape=[
            jax.ShapeDtypeStruct(whole, jnp.float32),
            jax.ShapeDtypeStruct(whole, jnp.float32),
            jax.ShapeDtypeStruct((2, 8, INNER), jnp.float32),
        ],
        in_specs=[pl.BlockSpec(memory_space=pl.ANY)] * 8,
        out_specs=[pl.BlockSpec(memory_space=pl.ANY)] * 3,
        scratch_shapes=[
            pltpu.VMEM((MODES, COMPS, 2, ROWS + 16, COLS), jnp.float32),
            pltpu.VMEM(whole, jnp.float32),
            pltpu.VMEM((COMPS, SPANS, 2, 8, COLS), jnp.float32),
            pltpu.VMEM((COMPS, SPANS, 2, 8, COLS), jnp.float32),
            pltpu.VMEM((OUTER, 8, 2 * INNER), jnp.float32),
            pltpu.VMEM((OUTER, 8, 2 * INNER), jnp.float32),
            pltpu.VMEM((2, 2, 2 * INNER, 2 * INNER), jnp.bfloat16),
            pltpu.VMEM((OUTER, 3, INNER), jnp.float32),
            pltpu.VMEM((STEN + 2, ROWS, INNER), jnp.float32),
            pltpu.VMEM((INNER, INNER), jnp.float32),
            pltpu.VMEM((2, ROWS), jnp.float32),
            pltpu.VMEM((STEN, ROWS), jnp.float32),
            pltpu.SMEM((2, 8), jnp.float32),
            pltpu.SMEM((MODES,), jnp.int32),
            pltpu.VMEM((1, COLS), jnp.int32),
            pltpu.VMEM((MODES, 2, 8, COLS), jnp.float32),
            pltpu.VMEM((3, 8, INNER), jnp.float32),
            pltpu.VMEM((SPANS, 8, INNER), jnp.float32),
            dma((8,)),
            dma,
            dma((COMPS,)),
            dma,
            dma((COMPS,)),
            dma((2,)),
            dma((2,)),
            dma,
            dma,
            dma,
            dma((2,)),
            dma((2,)),
            dma,
            pltpu.SemaphoreType.REGULAR,
        ],
        compiler_params=pltpu.CompilerParams(collective_id=0, has_side_effects=True, vmem_limit_bytes=16 * 2**20),
    )(*[pltpu.with_memory_space_constraint(jnp.asarray(array), pltpu.HBM) for array in arrays])
    new_field = base + spanwise
    wall_grad = grads[:, :, :PATCH].reshape(2, MODES, 2, PATCH)
    return new_field, wall_grad


def solution(mesh):
    return jax.shard_map(
        on_device,
        mesh=mesh,
        in_specs=(
            P(None, None, None, "wall", "span"),
            P(None, "wall"),
            P(None, "wall"),
            P(),
            P(),
            P("span"),
        ),
        out_specs=(P(None, None, None, "wall", "span"), P()),
        check_vma=False,
    )
```
